768 devices in a mesh: gx: 12 (over z), gy: 64 (over x, y, core).
Axes of the slice: x: 4, y: 8, z: 12, core: 2. Of those that a mesh axis runs over, the one named last changes fastest.
Arguments:
- wavefield: float32 [9, 56, 98304], P(None, None, ('gx', 'gy')), may hold values from -6 to 6
- star_mats: float32 [3, 9, 9, 98304], P(None, None, None, ('gx', 'gy')), may hold values from -1 to 1
- flux_own: float32 [4, 9, 9, 98304], P(None, None, None, ('gx', 'gy')), may hold values from -0.8 to 0.8
- flux_nbr: float32 [4, 9, 9, 98304], P(None, None, None, ('gx', 'gy')), may hold values from -0.8 to 0.8
- stiffness: float32 [3, 56, 56], replicated, may hold values from -0.75 to 0.75
- face_proj: float32 [4, 21, 56], replicated, may hold values from -0.75 to 0.75
- lift_mats: float32 [4, 56, 21], replicated, may hold values from -1.25 to 1.25
- cluster: int32 [98304], P(('gx', 'gy')), may hold values from 0 to 1
- yield_stress: float32 [98304], P(('gx', 'gy')), may hold values from 0.5 to 5
- plastic_mask: int32 [98304], P(('gx', 'gy')), may hold values from 0 to 1
- face_source: int32 [4, 98304], P(None, ('gx', 'gy')), may hold values from 0 to 639, as said below
- send_faces: int32 [3072, 32], P(('gx', 'gy')), may hold values from 0 to 511, as said below
- fault_faces: int32 [768, 64], P(('gx', 'gy')), may hold values from 0 to 511, as said below
- fault_owner: int32 [49152, 1], P(('gx', 'gy')), may hold values from 0 to 63; in each aligned block of 64 rows (0 to 63, 64 to 127, ...) at most 2 rows name the same one
- fault_slip: float32 [98304], P(('gx', 'gy')), may hold values from 0 to 1
- cohesion: float32 [98304], P(('gx', 'gy')), may hold values from 0.1 to 1
- slip_flag: int32 [98304], P(('gx', 'gy')), may hold values from 0 to 1
Outputs:
- wavefield_out: float32 [9, 56, 98304], P(None, None, ('gx', 'gy'))
- slip_out: float32 [98304], P(('gx', 'gy'))
The draws below stay inside these ranges and needn't reach their ends.
Inputs may be any that keep to these rules, and one draw needn't show every extreme that they name: `face_source`: entries below 512 name the partition's own faces; every received slot is named by exactly one face of its partition. `send_faces`: entries of one row are distinct. `fault_faces`: entries of one partition are distinct. `fault_owner`: among the fault faces of one partition at most 2 name the same owner.
All inputs are finite; a program needn't handle non-finite values.
Results may differ from the reference program's by a relative error of at most 0.0001.
Values sent between devices are 32-bit elements; how exact they have to be, the bound alone decides.
No kernel may reach another device: no remote copies, remote signals or barrier semaphores. Data moves between devices by JAX's collectives and lax.ppermute only.
A program may use at most 64 MiB of HBM per device.

```python
import math
import jax
import jax.numpy as jnp
import numpy as np
from jax import lax

VARS = 9
MODES = 56
FACE_PTS = 21
ORDER = 6
CYCLES = 1
E_DEV = 128
SLOTS = 32
FAULT_DEV = 64
PARTITIONS = 768
ELEMS = 98304
CAP = 2
OWNER_SLOTS = 98304
N_GX = 12
N_GY = 64


def face_rows(key):
    keys = jax.random.split(key, 2)
    shuffled = jax.random.permutation(keys[0], 4 * E_DEV).astype(jnp.int32)
    local_rows = jax.random.randint(keys[1], (4 * E_DEV,), 0, 4 * E_DEV).astype(jnp.int32)
    slot_rows = 4 * E_DEV + jnp.arange(4 * SLOTS, dtype=jnp.int32)
    return local_rows.at[shuffled[:4 * SLOTS]].set(slot_rows)


def topped_choice(key, amount):
    shuffled = jax.random.permutation(key, 4 * E_DEV).astype(jnp.int32)
    where_top = jnp.argmax(shuffled)
    leading = shuffled[0]
    shuffled = shuffled.at[where_top].set(leading).at[0].set(4 * E_DEV - 1)
    return shuffled[:amount]


def draw_face_source(key, part):
    keys = jax.random.split(jax.random.fold_in(key, 11), PARTITIONS)
    stacked = jax.vmap(face_rows)(keys)
    return jnp.transpose(stacked.reshape(PARTITIONS, 4, E_DEV), (1, 0, 2)).reshape(4, PARTITIONS * E_DEV).astype(jnp.int32)


def draw_send_faces(key, part):
    keys = jax.random.split(jax.random.fold_in(key, 23), PARTITIONS)
    stacked = jax.vmap(lambda single: topped_choice(single, 4 * SLOTS))(keys)
    return stacked.reshape(PARTITIONS * 4, SLOTS).astype(jnp.int32)


def draw_fault_faces(key, part):
    keys = jax.random.split(jax.random.fold_in(key, 37), PARTITIONS)
    stacked = jax.vmap(lambda single: topped_choice(single, FAULT_DEV))(keys)
    return stacked.reshape(PARTITIONS, FAULT_DEV).astype(jnp.int32)


def set_ends(entries, key, least, largest):
    longest = entries.shape.index(max(entries.shape))
    spots = []
    for shift in (0, 1):
        where = [jax.random.randint(jax.random.fold_in(key, axis), (), 0, length) for axis, length in enumerate(entries.shape)]
        where[longest] = (where[longest] + shift) % entries.shape[longest]
        spots.append(tuple(where))
    return entries.at[spots[0]].set(least).at[spots[1]].set(largest)


def level_of(rng, dims, shards, smallest, top_value):
    factor_of = 1.0
    for axis_at, blocks in shards:
        draws = jax.random.uniform(jax.random.fold_in(jax.random.fold_in(rng, 6), axis_at), (blocks,), jnp.float32, smallest / len(shards), top_value / len(shards))
        factor_of = factor_of * jnp.repeat(jnp.exp(draws), dims[axis_at] // blocks).reshape((-1,) + (1,) * (len(dims) - 1 - axis_at))
    return factor_of


def shared_out(own_key, own, number, rows, count, top, limit, slope):
    order = jax.random.permutation(own_key, count)
    crowded, usual = shares(count, rows * top, limit, slope, True), shares(count, rows * top, limit, slope, False)
    places = jnp.arange(count)

    def named(sizes, rotation):
        used = int((sizes > 0).sum())
        fixed = max(1, used // 4)
        moved = fixed + (places - fixed + rotation * (used - fixed)) % max(1, count - fixed)
        return jnp.zeros((count,), jnp.int32).at[order[jnp.where(places < fixed, places, moved)]].set(jnp.asarray(sizes, jnp.int32))

    sizes = jnp.where(number % 4 == 0, named(crowded, number // 4), named(usual, number - number // 4 - 1))
    mixed = jax.random.permutation(jax.random.fold_in(own, 3), count)
    donor, sink = mixed[0:count // 2 * 2:2], mixed[1:count // 2 * 2:2]
    room = jnp.minimum(sizes[donor] - 1, limit - sizes[sink]) // 2
    room = jnp.where((donor == order[0]) | (sink == order[0]) | (sizes[sink] == 0), 0, jnp.maximum(room, 0))
    moved = jax.random.randint(jax.random.fold_in(own, 4), (count // 2,), 0, 1 << 20) % (room + 1)
    sizes = sizes.at[donor].add(-moved).at[sink].add(moved)
    items = jnp.searchsorted(jnp.cumsum(sizes), jnp.arange(rows * top), side="right").astype(jnp.int32)
    grid = items.reshape(top, rows).T
    grid = grid[jax.random.permutation(jax.random.fold_in(own, 1), rows)]
    rotation = jax.random.randint(jax.random.fold_in(own, 2), (rows, 1), 0, top)
    return jnp.take_along_axis(grid, (jnp.arange(top)[None, :] + rotation) % top, axis=1)


def shares(number_of, total, most, lean, full):
    loads = [(1 << 20) // math.isqrt(grade ** lean) + 1 for grade in range(1, number_of + 1)]
    largest = most if full else min(most, max(-(-total // number_of), total * loads[0] // sum(loads)))
    least = 1 if total - largest >= number_of - 1 else 0
    given, surplus = [largest] + [least] * (number_of - 1), total - largest - least * (number_of - 1)
    while surplus > 0:
        free = [i for i in range(1, number_of) if given[i] < largest] or [i for i in range(1, number_of) if given[i] < most]
        mass, budget = sum([loads[i] for i in free]), surplus
        for i in free:
            extra = min(most - given[i], max(1, budget * loads[i] // mass), surplus)
            given[i] = given[i] + extra
            surplus = surplus - extra
    return np.array(given)


def centred(stream_key, dims, scale, most, cuts=(), held_as=jnp.bfloat16):
    values = jax.random.normal(stream_key, dims, jnp.float32) * scale
    if len(cuts) > 0:
        values = level_of(stream_key, dims, cuts, -0.22, 0.18) * values
    return jnp.clip(values, min=-most, max=most).astype(held_as)


def setup_inputs(seed: int = 0) -> dict:
    arg_keys = jax.random.split(jax.random.key(seed), 18)
    wavefield = centred(arg_keys[0], (VARS, MODES, ELEMS), 1.0, 6.0, ((2, 768),), jnp.float32)
    star_mats = centred(arg_keys[1], (3, VARS, VARS, ELEMS), 0.15, 1.0, ((3, 768),), jnp.float32)
    flux_own = centred(arg_keys[2], (4, VARS, VARS, ELEMS), 0.1, 0.8, ((3, 768),), jnp.float32)
    flux_nbr = centred(arg_keys[3], (4, VARS, VARS, ELEMS), 0.1, 0.8, ((3, 768),), jnp.float32)
    stiffness = centred(arg_keys[4], (3, MODES, MODES), MODES ** -0.5, 0.75, (), jnp.float32)
    face_proj = centred(arg_keys[5], (4, FACE_PTS, MODES), MODES ** -0.5, 0.75, (), jnp.float32)
    lift_mats = centred(arg_keys[6], (4, MODES, FACE_PTS), FACE_PTS ** -0.5, 1.25, (), jnp.float32)
    cluster = set_ends(jax.random.randint(arg_keys[7], (ELEMS,), 0, 2), jax.random.fold_in(arg_keys[7], 1), 0, 1).astype(jnp.int32)
    yield_stress = jnp.clip(jnp.exp(math.log(5.0) - 2.3025851 * jax.random.uniform(arg_keys[8], (ELEMS,), jnp.float32) ** level_of(arg_keys[8], (ELEMS,), ((0, 768),), -0.2, 0.2)), 0.5, 5.0)
    plastic_mask = set_ends(jax.random.randint(arg_keys[9], (ELEMS,), 0, 2), jax.random.fold_in(arg_keys[9], 1), 0, 1).astype(jnp.int32)
    face_source = draw_face_source(jax.random.fold_in(arg_keys[17], 71), 0)
    send_faces = draw_send_faces(jax.random.fold_in(arg_keys[17], 71), 0)
    fault_faces = draw_fault_faces(jax.random.fold_in(arg_keys[17], 71), 0)
    fault_owner_keys = jax.random.split(jax.random.fold_in(arg_keys[13], 1), (PARTITIONS * FAULT_DEV) // FAULT_DEV)
    fault_owner_turns = jax.random.permutation(jax.random.fold_in(arg_keys[13], 3), (PARTITIONS * FAULT_DEV) // FAULT_DEV)
    fault_owner = jax.vmap(lambda own, number: shared_out(jax.random.fold_in(arg_keys[13], 2), own, number, FAULT_DEV, N_GY, 1, CAP, 2))(fault_owner_keys, fault_owner_turns).reshape((PARTITIONS * FAULT_DEV, 1))
    fault_slip = jnp.clip(1.0 * jax.random.uniform(arg_keys[14], (OWNER_SLOTS,), jnp.float32) ** level_of(arg_keys[14], (OWNER_SLOTS,), ((0, 768),), -0.2, 0.2), 0.0, 1.0)
    cohesion = jnp.clip(jnp.exp(math.log(1.0) - 2.3025851 * jax.random.uniform(arg_keys[15], (OWNER_SLOTS,), jnp.float32) ** level_of(arg_keys[15], (OWNER_SLOTS,), ((0, 768),), -0.2, 0.2)), 0.1, 1.0)
    slip_flag = set_ends(jax.random.randint(arg_keys[16], (OWNER_SLOTS,), 0, 2), jax.random.fold_in(arg_keys[16], 1), 0, 1).astype(jnp.int32)
    return dict(wavefield=wavefield, star_mats=star_mats, flux_own=flux_own, flux_nbr=flux_nbr, stiffness=stiffness, face_proj=face_proj, lift_mats=lift_mats, cluster=cluster, yield_stress=yield_stress, plastic_mask=plastic_mask, face_source=face_source, send_faces=send_faces, fault_faces=fault_faces, fault_owner=fault_owner, fault_slip=fault_slip, cohesion=cohesion, slip_flag=slip_flag)


highest = lax.Precision.HIGHEST
picked_vars = (0, 3, 5, 6, 7, 8)

def vars_mix(mats, field):
    total = mats[:, 0][:, None] * field[0][None]
    for source in range(1, field.shape[0]):
        total = total + mats[:, source][:, None] * field[source][None]
    return total

def face_mix(mats_one, trace_one, mats_two, trace_two):
    total = 0.0
    for source in range(trace_one.shape[0]):
        left = jnp.transpose(mats_one[:, :, source], (1, 0, 2))[:, None]
        right = jnp.transpose(mats_two[:, :, source], (1, 0, 2))[:, None]
        total = total + left * trace_one[source][None] + right * trace_two[source][None]
    return total

def predict(wavefield, star_mats, stiffness):
    deriv = wavefield
    early = wavefield
    late = wavefield
    factor = 1.0
    for power in range(2, ORDER + 1):
        factor = factor * power
        change = 0.0
        for axis_dir in range(3):
            mixed = vars_mix(star_mats[axis_dir], deriv)
            change = change + jnp.einsum('nm,vmx->vnx', stiffness[axis_dir], mixed, precision=highest)
        deriv = -change
        early = early + deriv / factor
        late = late + deriv * ((2.0 ** power - 1.0) / factor)
    return (early, late)

def volume(integral, star_mats, stiffness):
    total = 0.0
    for axis_dir in range(3):
        mixed = vars_mix(star_mats[axis_dir], integral)
        total = total + jnp.einsum('mn,vmx->vnx', stiffness[axis_dir], mixed, precision=highest)
    return total

def godunov(picked):
    stacked = []
    for component in range(3):
        stacked.append(0.5 * (picked[component] + picked[6 + component]) + 0.5 * (picked[9 + component] - picked[3 + component]))
    return jnp.stack(stacked)

def friction(state, slip_state, cohesion, slip_flag):
    weaken = jnp.minimum(slip_state / 0.5, 1.0)
    coeff = 0.6 - 0.3 * weaken
    strength = cohesion + coeff * jnp.maximum(-state[0], 0.0)
    magnitude = jnp.sqrt(state[1] * state[1] + state[2] * state[2])
    ratio = jnp.where(slip_flag == 1, strength / jnp.maximum(magnitude, strength), 1.0)
    change = jnp.stack([state[1] * (ratio - 1.0), state[2] * (ratio - 1.0)])
    slip_new = slip_state + lax.optimization_barrier(jnp.mean(magnitude * (1.0 - ratio), axis=0))
    return (change, slip_new)

def plastic(wavefield, plastic_mask, yield_stress):
    mean_stress = (wavefield[0] + wavefield[1] + wavefield[2]) / 3.0
    deviator = wavefield[0:3] - mean_stress
    shear = wavefield[3:6]
    second = (lax.optimization_barrier(jnp.sum(deviator * deviator, axis=(0, 1))) + 2.0 * lax.optimization_barrier(jnp.sum(shear * shear, axis=(0, 1)))) / (2.0 * wavefield.shape[1])
    equiv = jnp.sqrt(second + 1e-06)
    factor = 1.0 - plastic_mask.astype(jnp.float32) * 0.5 * jnp.maximum(1.0 - yield_stress / equiv, 0.0)
    return jnp.concatenate([mean_stress + factor * deviator, factor * shear, wavefield[6:]], axis=0)

def reference(wavefield, star_mats, flux_own, flux_nbr, stiffness, face_proj, lift_mats, cluster, yield_stress, plastic_mask, face_source, send_faces, fault_faces, fault_owner, fault_slip, cohesion, slip_flag):
    parts = N_GX * N_GY
    elems = E_DEV
    width = VARS * FACE_PTS
    is_fine = (cluster == 0)[None, None, :]
    is_coarse = (cluster == 1)[None, None, :]
    owners = fault_owner[:, 0].reshape(parts, FAULT_DEV)
    onehot = (owners[:, :, None] == jnp.arange(N_GY, dtype=jnp.int32)[None, None, :]).astype(jnp.int32)
    before = jnp.cumsum(onehot, axis=1) - onehot
    order_rank = lax.optimization_barrier(jnp.sum(before * onehot, axis=2))
    row_x = (jnp.arange(parts, dtype=jnp.int32) // N_GY)[:, None]
    row_y = (jnp.arange(parts, dtype=jnp.int32) % N_GY)[:, None]
    slot_ids = ((row_x * N_GY + owners) * (N_GY * CAP) + row_y * CAP + order_rank).reshape(-1)
    face_index = fault_faces // elems
    elem_index = jnp.arange(parts, dtype=jnp.int32)[:, None] * elems + fault_faces % elems
    sources = face_source.reshape(4, parts, elems).transpose(1, 0, 2).reshape(parts, 4 * elems)
    sends = send_faces.reshape(parts, 4 * SLOTS)
    chosen = jnp.array(picked_vars, dtype=jnp.int32)

    def advance(integral, slip_state):
        own_traces = jnp.einsum('fjm,vmx->vjfx', face_proj, integral, precision=highest)
        own_table = own_traces.reshape(width, 4, parts, elems).transpose(0, 2, 1, 3).reshape(width, parts, 4 * elems)
        outgoing = jnp.take_along_axis(own_table, sends[None], axis=2).reshape(width, N_GX, N_GY, 4, SLOTS)
        received = jnp.stack([jnp.roll(outgoing[..., 1, :], 1, axis=1), jnp.roll(outgoing[..., 0, :], -1, axis=1), jnp.roll(outgoing[..., 3, :], 1, axis=2), jnp.roll(outgoing[..., 2, :], -1, axis=2)], axis=3)
        table = jnp.concatenate([own_table, received.reshape(width, parts, 4 * SLOTS)], axis=2)
        nbr_table = jnp.take_along_axis(table, sources[None], axis=2)
        nbr_traces = nbr_table.reshape(VARS, FACE_PTS, parts, 4, elems).transpose(0, 1, 3, 2, 4).reshape(VARS, FACE_PTS, 4, parts * elems)
        flux = face_mix(flux_own, own_traces, flux_nbr, nbr_traces)
        minus_side = jnp.take_along_axis(own_table, fault_faces[None], axis=2).reshape(VARS, FACE_PTS, parts * FAULT_DEV)
        plus_side = jnp.take_along_axis(nbr_table, fault_faces[None], axis=2).reshape(VARS, FACE_PTS, parts * FAULT_DEV)
        picked = jnp.concatenate([minus_side[chosen], plus_side[chosen]], axis=0)
        state = godunov(picked)
        slot_state = jnp.zeros((3, FACE_PTS, OWNER_SLOTS), jnp.float32).at[:, :, slot_ids].set(state)
        change, slip_new = friction(slot_state, slip_state, cohesion, slip_flag)
        back = change[:, :, slot_ids].reshape(2, FACE_PTS, parts, FAULT_DEV)
        flux = flux.at[3, :, face_index, elem_index].add(jnp.transpose(back[0], (1, 2, 0)))
        flux = flux.at[5, :, face_index, elem_index].add(jnp.transpose(back[1], (1, 2, 0)))
        increment = volume(integral, star_mats, stiffness) - jnp.einsum('fmj,vjfx->vmx', lift_mats, flux, precision=highest)
        return (increment, slip_new)
    slip_state = fault_slip
    for cycle_index in range(CYCLES):
        early, late = predict(wavefield, star_mats, stiffness)
        first_step, slip_state = advance(early, slip_state)
        carried = jnp.where(is_coarse, first_step, 0.0)
        midway = jnp.where(is_fine, plastic(wavefield + first_step, plastic_mask, yield_stress), wavefield)
        renewed, unused = predict(midway, star_mats, stiffness)
        second_step, slip_state = advance(jnp.where(is_coarse, late, renewed), slip_state)
        wavefield = plastic(midway + second_step + carried, plastic_mask, yield_stress)
    return (wavefield, slip_state)
```

```python
import jax
import jax.numpy as jnp
from jax import lax
from jax.experimental import pallas as pl
from jax.experimental.pallas import tpu as pltpu
from jax.sharding import PartitionSpec as P

F32 = jnp.float32
BF16 = jnp.bfloat16

VARS = 9
MODES = 56
FACE_PTS = 21
ORDER = 6
FACES = 4
E = 128
SLOTS = 32
PTS = 24
ROWS = 224
MSG = ROWS // 4
WIDE = VARS * E


def halves(x):
    top = x.astype(BF16)
    return top, (x - top.astype(F32)).astype(BF16)


def dot(a, b):
    return jnp.dot(a, b, preferred_element_type=F32)


def iota(shape, dim):
    return lax.broadcasted_iota(jnp.int32, shape, dim)


def one_hot(mask):
    return jnp.where(mask, 1.0, 0.0).astype(BF16)


def lanes(w):
    return slice(E * w, E * (w + 1))


def widen(x):
    top = x.astype(BF16).astype(F32)
    rest = x - top
    pair = [part + pltpu.roll(part, 64, 1) for part in (top, rest)]
    return jnp.concatenate(pair, axis=1).astype(BF16)


def stack_stiffness(stiff_ref, tall_ref):
    tall_ref[...] = jnp.zeros_like(tall_ref)
    for d in range(3):
        tall_ref[MODES * d : MODES * (d + 1), 0:MODES] = stiff_ref[d]
    return widen(tall_ref[...])


def stack_stiffness_t(stiff_ref, tall_ref, square_ref):
    square_ref[...] = jnp.zeros_like(square_ref)
    for d in range(3):
        square_ref[0:MODES, 0:MODES] = stiff_ref[d]
        tall_ref[MODES * d : MODES * (d + 1), :] = jnp.transpose(square_ref[...])[0:MODES]
    return widen(tall_ref[...])


def spread_faces(face_ref, square_ref):
    square_ref[...] = jnp.zeros_like(square_ref)
    for f in range(FACES):
        for j in range(FACE_PTS):
            square_ref[PTS * f + j : PTS * f + j + 1, 0:MODES] = face_ref[j, f : f + 1, :]


def load_rhs(read, rhs_ref):
    pad = jnp.zeros((64 - MODES, E), F32)
    for w in range(VARS):
        x = read(w)
        top = x.astype(BF16).astype(F32)
        high = jnp.concatenate([top, pad], axis=0).astype(BF16)
        low = jnp.concatenate([x - top, pad], axis=0).astype(BF16)
        rhs_ref[0:64, lanes(w)] = high
        rhs_ref[64:128, lanes(w)] = low
        rhs_ref[128:192, lanes(w)] = high
        rhs_ref[192:256, lanes(w)] = low


def product(a, rhs_ref, out_ref):
    for start in range(0, WIDE, 256):
        cols = slice(start, min(start + 256, WIDE))
        out_ref[:, cols] = dot(a, rhs_ref[:, cols])


def star_mix(star_ref, tall_ref, emit):
    def body(group, carry):
        sums = [jnp.zeros((MODES, E), F32) for _ in range(3)]
        for w in range(VARS):
            for d in range(3):
                x = tall_ref[MODES * d : MODES * (d + 1), lanes(w)]
                for i in range(3):
                    sums[i] = sums[i] + star_ref[3 * group + i, w, d : d + 1, :] * x
        for i in range(3):
            emit(3 * group + i, sums[i])
        return carry

    lax.fori_loop(0, 3, body, 0)


def predict(start_ref, star_ref, left, deriv_ref, rhs_ref, tall_ref, early_ref, late_ref):
    early_ref[...] = start_ref[...]
    if late_ref is not None:
        late_ref[...] = start_ref[...]
    factor = 1.0
    for power in range(2, ORDER + 1):
        factor = factor * power
        source = start_ref if power == 2 else deriv_ref
        load_rhs(lambda w: source[w], rhs_ref)
        product(left, rhs_ref, tall_ref)
        to_early = 1.0 / factor
        to_late = (2.0**power - 1.0) / factor

        def emit(v, change):
            if power < ORDER:
                deriv_ref[v] = -change
            early_ref[v] = early_ref[v] - change * to_early
            if late_ref is not None:
                late_ref[v] = late_ref[v] - change * to_late

        star_mix(star_ref, tall_ref, emit)


def direction_rows(send_ref):
    rows = [send_ref[d : d + 1, :] for d in range(4)]
    order = []
    for axis, base in (("gx", 0), ("gy", 2)):
        odd = lax.axis_index(axis) % 2 == 1
        order.append(jnp.where(odd, rows[base], rows[base + 1]))
        order.append(jnp.where(odd, rows[base + 1], rows[base]))
    return order


def make_traces(left, integral_ref, rhs_ref, own_ref, table_ref, high_ref, low_ref):
    load_rhs(lambda w: integral_ref[w], rhs_ref)
    product(left, rhs_ref, own_ref)
    for w in range(VARS):
        for f in range(FACES):
            table_ref[PTS * w : PTS * (w + 1), lanes(f)] = own_ref[PTS * f : PTS * (f + 1), lanes(w)]
    table_ref[PTS * VARS : ROWS, :] = jnp.zeros((ROWS - PTS * VARS, FACES * E), F32)
    high, low = halves(table_ref[...])
    high_ref[...] = high
    low_ref[...] = low


def make_messages(send_ref, high_ref, low_ref, out_refs):
    listed = jnp.concatenate(direction_rows(send_ref), axis=1)
    pick = one_hot(iota((FACES * E, 4 * SLOTS), 0) == listed)
    picked = dot(high_ref[...], pick) + dot(low_ref[...], pick)
    turned = [picked] + [pltpu.roll(picked, SLOTS * k, 1) for k in range(1, 4)]
    part = iota((MSG, E), 1) // SLOTS
    for b in range(4):
        packed = turned[(0 - b) % 4][0:MSG]
        for q in range(1, 4):
            packed = jnp.where(part == q, turned[(q - b) % 4][MSG * q : MSG * (q + 1)], packed)
        out_refs[b][...] = packed


def unpack_messages(in_refs):
    part = iota((MSG, E), 1) // SLOTS
    blocks = []
    for q in range(4):
        block = None
        for b in range(4):
            shift = (SLOTS * (b - q)) % E
            x = in_refs[b][...]
            x = pltpu.roll(x, shift, 1) if shift else x
            block = x if block is None else jnp.where(part == b, x, block)
        blocks.append(block)
    return jnp.concatenate(blocks, axis=0)


def received_slots(source_ref):
    slot = source_ref[...] - FACES * E
    swap_x = SLOTS * (1 - lax.axis_index("gx") % 2)
    swap_y = SLOTS * (1 - lax.axis_index("gy") % 2)
    swap = jnp.where(slot < 2 * SLOTS, swap_x, swap_y)
    return jnp.where(slot < 0, slot, slot ^ swap)


def finish_gather(source_ref, message_refs, near_ref, nbr_ref):
    slots = received_slots(source_ref)
    high, low = halves(unpack_messages(message_refs))
    for f in range(FACES):
        pick = one_hot(iota((4 * SLOTS, E), 0) == slots[f : f + 1])
        far = dot(high, pick) + dot(low, pick)
        nbr_ref[:, lanes(f)] = near_ref[:, lanes(f)] + far


def face_state(own_ref, nbr_ref, faces_row, state_ref):
    for c, (t, s) in enumerate(((0, 6), (3, 7), (5, 8))):
        for f in range(FACES):
            own_t = own_ref[PTS * f : PTS * (f + 1), lanes(t)]
            own_v = own_ref[PTS * f : PTS * (f + 1), lanes(s)]
            nbr_t = nbr_ref[PTS * t : PTS * (t + 1), lanes(f)]
            nbr_v = nbr_ref[PTS * s : PTS * (s + 1), lanes(f)]
            state_ref[PTS * c : PTS * (c + 1), lanes(f)] = 0.5 * (own_t + nbr_t) + 0.5 * (nbr_v - own_v)
    high, low = halves(state_ref[...])
    pick = one_hot(iota((FACES * E, faces_row.shape[1]), 0) == faces_row)
    return dot(high, pick) + dot(low, pick)


def column_of(row):
    count = row.shape[1]
    diagonal = iota((count, count), 0) == iota((count, count), 1)
    return jnp.sum(jnp.where(diagonal, row.astype(F32), 0.0), axis=1, keepdims=True)


def owner_masks(owner_row, gy_size):
    count = owner_row.shape[1]
    owner_col = column_of(owner_row)
    same = owner_col == owner_row.astype(F32)
    earlier = iota((count, count), 0) < iota((count, count), 1)
    rank = jnp.sum(jnp.where(same & earlier, 1.0, 0.0), axis=0, keepdims=True)
    named = iota((gy_size, count), 0) == owner_row
    return named, rank


def slot_values(params_ref, named, rank):
    out = []
    for c in range(3):
        both = []
        for r in range(2):
            col = params_ref[:, 3 * r + c : 3 * r + c + 1]
            both.append(jnp.sum(jnp.where(named, col, 0.0), axis=0, keepdims=True))
        out.append(jnp.where(rank > 0.5, both[1], both[0]))
    return out


def friction(state, slip, cohesion, flag):
    coeff = 0.6 - 0.3 * jnp.minimum(slip / 0.5, 1.0)
    normal, first, second = (state[PTS * c : PTS * (c + 1)] for c in range(3))
    strength = cohesion + coeff * jnp.maximum(-normal, 0.0)
    magnitude = jnp.sqrt(first * first + second * second)
    ratio = jnp.where(flag > 0.5, strength / jnp.maximum(magnitude, strength), 1.0)
    change = jnp.concatenate([first * (ratio - 1.0), second * (ratio - 1.0)], axis=0)
    slip_new = slip + jnp.sum(magnitude * (1.0 - ratio), axis=0, keepdims=True) / FACE_PTS
    return change, slip_new


def spread_change(change, faces_row):
    count = faces_row.shape[1]
    faces_col = column_of(faces_row)
    place = one_hot(iota((count, FACES * E), 1).astype(F32) == faces_col)
    high, low = halves(change)
    return dot(high, place) + dot(low, place)


def mix_faces(mats_ref, trace, start, flux_ref):
    def body(v, carry):
        cols = pl.ds(pl.multiple_of(v * E, E), E)
        for f in range(FACES):
            rows = slice(PTS * f, PTS * (f + 1))
            total = None if start is None else start[rows, cols]
            for w in range(VARS):
                term = mats_ref[v, w, f : f + 1, :] * trace(f, w)
                total = term if total is None else total + term
            flux_ref[rows, cols] = total
        return carry

    lax.fori_loop(0, VARS, body, 0)


def lift(lift_ref, flux_ref, out_ref):
    top = lift_ref[0][:, 0 : FACES * PTS]
    rest = lift_ref[1][:, 0 : FACES * PTS]
    for start in range(0, WIDE, 256):
        cols = slice(start, min(start + 256, WIDE))
        high, low = halves(flux_ref[:, cols])
        out_ref[:, cols] = dot(top, high) + (dot(top, low) + dot(rest, high))


def add_change(flux_ref, delta):
    for c, v in ((0, 3), (1, 5)):
        for f in range(FACES):
            rows = slice(PTS * f, PTS * (f + 1))
            flux_ref[rows, lanes(v)] = flux_ref[rows, lanes(v)] + delta[PTS * c : PTS * (c + 1), lanes(f)]


def plastic(read, mask_row, yield_row):
    q = [read(v) for v in range(6)]
    mean = (q[0] + q[1] + q[2]) / 3.0
    dev = [x - mean for x in q[0:3]]
    dev_sq = dev[0] * dev[0] + dev[1] * dev[1] + dev[2] * dev[2]
    shear_sq = q[3] * q[3] + q[4] * q[4] + q[5] * q[5]
    second = jnp.sum(dev_sq + 2.0 * shear_sq, axis=0, keepdims=True) / (2.0 * MODES)
    equiv = jnp.sqrt(second + 1e-06)
    factor = 1.0 - mask_row.astype(F32) * 0.5 * jnp.maximum(1.0 - yield_row / equiv, 0.0)
    return [mean + factor * x for x in dev] + [factor * x for x in q[3:6]]


def params_kernel(slip_ref, cohesion_ref, flag_ref, out_ref):
    gy_size = out_ref.shape[0]
    shape = (gy_size, slip_ref.shape[1])
    cols = []
    for r in range(2):
        mine = iota(shape, 1) == 2 * iota(shape, 0) + r
        for row in (slip_ref[...], cohesion_ref[...], flag_ref[...].astype(F32)):
            cols.append(jnp.sum(jnp.where(mine, row, 0.0), axis=1, keepdims=True))
    column = iota(out_ref.shape, 1)
    out = jnp.zeros(out_ref.shape, F32)
    for i, col in enumerate(cols):
        out = jnp.where(column == i, col, out)
    out_ref[...] = out


def slip_kernel(in_ref, out_ref):
    shape = (in_ref.shape[0], out_ref.shape[1])
    out = jnp.zeros((1, shape[1]), F32)
    for r in range(2):
        mine = iota(shape, 1) == 2 * iota(shape, 0) + r
        out = out + jnp.sum(jnp.where(mine, in_ref[:, r : r + 1], 0.0), axis=0, keepdims=True)
    out_ref[...] = out


def first_kernel(
    wave_ref, star_ref, stiff_ref, proj_ref, send_ref,
    early_ref, late_ref, own_ref, high_ref, low_ref, m0, m1, m2, m3, ap_ref, at_ref,
    deriv_ref, rhs_ref, tall_ref, lhs_ref, square_ref, table_ref,
):
    ap_ref[...] = stack_stiffness(stiff_ref, lhs_ref)
    spread_faces(proj_ref, square_ref)
    at_ref[...] = widen(square_ref[0 : FACES * PTS])
    predict(wave_ref, star_ref, ap_ref[...], deriv_ref, rhs_ref, tall_ref, early_ref, late_ref)
    make_traces(at_ref[...], early_ref, rhs_ref, own_ref, table_ref, high_ref, low_ref)
    make_messages(send_ref, high_ref, low_ref, (m0, m1, m2, m3))


def near_work(integral_ref, star_ref, own_mats_ref, own_ref, high_ref, low_ref, source_ref, left,
              vol_ref, flux_ref, near_ref, rhs_ref, tall_ref):
    load_rhs(lambda w: integral_ref[w], rhs_ref)
    product(left, rhs_ref, tall_ref)

    def emit(v, total):
        vol_ref[v] = total

    star_mix(star_ref, tall_ref, emit)
    mix_faces(own_mats_ref, lambda f, w: own_ref[PTS * f : PTS * (f + 1), lanes(w)], None, flux_ref)
    for f in range(FACES):
        pick = one_hot(iota((FACES * E, E), 0) == source_ref[f : f + 1, :])
        near_ref[:, lanes(f)] = dot(high_ref[...], pick) + dot(low_ref[...], pick)


def near_first_kernel(
    integral_ref, star_ref, own_mats_ref, own_ref, high_ref, low_ref, source_ref, stiff_ref, lift_ref,
    vol_ref, flux_ref, near_ref, av_ref, al_ref,
    rhs_ref, tall_ref, lhs_ref, square_ref,
):
    av_ref[...] = stack_stiffness_t(stiff_ref, lhs_ref, square_ref)
    spread_faces(lift_ref, square_ref)
    high, low = halves(jnp.transpose(square_ref[...])[0:MODES])
    al_ref[0] = high
    al_ref[1] = low
    near_work(integral_ref, star_ref, own_mats_ref, own_ref, high_ref, low_ref, source_ref, av_ref[...],
              vol_ref, flux_ref, near_ref, rhs_ref, tall_ref)


def near_second_kernel(
    integral_ref, star_ref, own_mats_ref, own_ref, high_ref, low_ref, source_ref, av_ref,
    vol_ref, flux_ref, near_ref,
    rhs_ref, tall_ref,
):
    near_work(integral_ref, star_ref, own_mats_ref, own_ref, high_ref, low_ref, source_ref, av_ref[...],
              vol_ref, flux_ref, near_ref, rhs_ref, tall_ref)


def middle_kernel(
    wave_ref, late_ref, vol_ref, part_ref, near_ref, own_ref, m0, m1, m2, m3, nbr_mats_ref, source_ref,
    faces_ref, owner_ref, params_ref, star_ref, ap_ref, at_ref, al_ref, send_ref, cluster_ref, yield_ref, mask_ref,
    integral_ref, base_ref, own2_ref, high_ref, low_ref, n0, n1, n2, n3, par_ref,
    nbr_ref, state_ref, flux_ref, lifted_ref, mid_ref, deriv_ref, rhs_ref, tall_ref, table_ref,
):
    finish_gather(source_ref, (m0, m1, m2, m3), near_ref, nbr_ref)
    faces_row = faces_ref[...]
    state = face_state(own_ref, nbr_ref, faces_row, state_ref)
    named, rank = owner_masks(owner_ref[...], params_ref.shape[0])
    slip, cohesion, flag = slot_values(params_ref, named, rank)
    change, slip_new = friction(state, slip, cohesion, flag)
    par_ref[0:1, :] = slip_new
    par_ref[1:2, :] = cohesion
    par_ref[2:3, :] = flag
    delta = spread_change(change, faces_row)
    mix_faces(
        nbr_mats_ref, lambda f, w: nbr_ref[PTS * w : PTS * (w + 1), lanes(f)], part_ref, flux_ref
    )
    add_change(flux_ref, delta)
    lift(al_ref, flux_ref, lifted_ref)
    coarse = cluster_ref[...] == 1
    for v in range(VARS):
        increment = vol_ref[v] - lifted_ref[:, lanes(v)]
        mid_ref[v] = wave_ref[v] + increment
        base_ref[v] = jnp.where(coarse, increment, 0.0)
    stressed = plastic(lambda v: mid_ref[v], mask_ref[...], yield_ref[...])
    for v in range(VARS):
        fine = stressed[v] if v < 6 else mid_ref[v]
        midway = jnp.where(coarse, wave_ref[v], fine)
        mid_ref[v] = midway
        base_ref[v] = midway + base_ref[v]
    predict(mid_ref, star_ref, ap_ref[...], deriv_ref, rhs_ref, tall_ref, integral_ref, None)
    for v in range(VARS):
        integral_ref[v] = jnp.where(coarse, late_ref[v], integral_ref[v])
    make_traces(at_ref[...], integral_ref, rhs_ref, own2_ref, table_ref, high_ref, low_ref)
    make_messages(send_ref, high_ref, low_ref, (n0, n1, n2, n3))


def fault_kernel(
    near_ref, own_ref, m0, m1, m2, m3, source_ref, faces_ref, owner_ref, params_ref, par_ref,
    nbr_ref, delta_ref, back_ref,
    state_ref,
):
    finish_gather(source_ref, (m0, m1, m2, m3), near_ref, nbr_ref)
    faces_row = faces_ref[...]
    state = face_state(own_ref, nbr_ref, faces_row, state_ref)
    change, slip_new = friction(state, par_ref[0:1, :], par_ref[1:2, :], par_ref[2:3, :])
    delta_ref[...] = spread_change(change, faces_row)
    named, rank = owner_masks(owner_ref[...], params_ref.shape[0])
    column = iota(back_ref.shape, 1)
    out = jnp.zeros(back_ref.shape, F32)
    for r in range(2):
        here = named & ((rank > 0.5) == (r == 1))
        total = jnp.sum(jnp.where(here, slip_new, 0.0), axis=1, keepdims=True)
        used = jnp.sum(jnp.where(here, 1.0, 0.0), axis=1, keepdims=True)
        value = jnp.where(used > 0.5, total, params_ref[:, 3 * r : 3 * r + 1])
        out = jnp.where(column == r, value, out)
    back_ref[...] = out


def last_kernel(
    base_ref, vol_ref, part_ref, nbr_ref, delta_ref, nbr_mats_ref, al_ref, yield_ref, mask_ref,
    out_ref,
    flux_ref, lifted_ref,
):
    mix_faces(
        nbr_mats_ref, lambda f, w: nbr_ref[PTS * w : PTS * (w + 1), lanes(f)], part_ref, flux_ref
    )
    add_change(flux_ref, delta_ref[...])
    lift(al_ref, flux_ref, lifted_ref)
    for v in range(VARS):
        out_ref[v] = base_ref[v] + (vol_ref[v] - lifted_ref[:, lanes(v)])
    stressed = plastic(lambda v: out_ref[v], mask_ref[...], yield_ref[...])
    for v in range(6):
        out_ref[v] = stressed[v]


def shape(dims, dtype=F32):
    return jax.ShapeDtypeStruct(dims, dtype)


def call(kernel, outs, scratch=()):
    return pl.pallas_call(
        kernel,
        out_shape=outs,
        scratch_shapes=[pltpu.VMEM(dims, dtype) for dims, dtype in scratch],
    )


FIELD = (VARS, MODES, E)
TRACE = (FACES * PTS, WIDE)
TABLE = (ROWS, FACES * E)
LEFT = (3 * MODES, 256)
TALL = (3 * MODES, WIDE)
RHS = (256, WIDE)


def pair_up(x, axis, odd):
    count = lax.axis_size(axis)
    if odd:
        pairs = [(i, (i + 1) % count if i % 2 else (i - 1) % count) for i in range(count)]
    else:
        pairs = [(i, i ^ 1) for i in range(count)]
    return lax.ppermute(x, axis, pairs)


def exchange(messages):
    return [pair_up(x, axis, odd) for x, (axis, odd) in zip(messages, (("gx", 0), ("gx", 1), ("gy", 0), ("gy", 1)))]


def local(
    wavefield,
    star_mats,
    flux_own,
    flux_nbr,
    stiffness,
    face_proj,
    lift_mats,
    cluster,
    yield_stress,
    plastic_mask,
    face_source,
    send_faces,
    fault_faces,
    fault_owner,
    fault_slip,
    cohesion,
    slip_flag,
):
    gy_size = lax.axis_size("gy")
    faults = fault_faces.shape[1]
    slot_count = fault_slip.shape[0]
    star = jnp.transpose(star_mats, (1, 2, 0, 3))
    own_mats = jnp.transpose(flux_own, (1, 2, 0, 3))
    nbr_mats = jnp.transpose(flux_nbr, (1, 2, 0, 3))
    proj = jnp.transpose(face_proj, (1, 0, 2))
    lifts = jnp.transpose(lift_mats, (2, 0, 1))
    owner = jnp.transpose(fault_owner)
    cluster, yield_stress, plastic_mask = (x.reshape(1, E) for x in (cluster, yield_stress, plastic_mask))
    slots = [x.reshape(1, slot_count) for x in (fault_slip, cohesion, slip_flag)]

    params = call(params_kernel, shape((gy_size, 8)))(*slots)
    params = lax.all_to_all(params, "gy", 0, 0, tiled=True)

    messages = [shape((MSG, E))] * 4
    work = [(FIELD, F32), (RHS, BF16), (TALL, F32)]
    early, late, own, high, low, m0, m1, m2, m3, ap, at = call(
        first_kernel,
        [shape(FIELD), shape(FIELD), shape(TRACE), shape(TABLE, BF16), shape(TABLE, BF16), *messages,
         shape(LEFT, BF16), shape((FACES * PTS, 256), BF16)],
        work + [((3 * MODES, E), F32), ((E, E), F32), (TABLE, F32)],
    )(wavefield, star, stiffness, proj, send_faces)
    got = exchange((m0, m1, m2, m3))
    vol, part, near, av, al = call(
        near_first_kernel,
        [shape(FIELD), shape(TRACE), shape(TABLE), shape(LEFT, BF16), shape((2, MODES, E), BF16)],
        work[1:] + [((3 * MODES, E), F32), ((E, E), F32)],
    )(early, star, own_mats, own, high, low, face_source, stiffness, lifts)
    integral, base, own, high, low, m0, m1, m2, m3, par = call(
        middle_kernel,
        [shape(FIELD), shape(FIELD), shape(TRACE), shape(TABLE, BF16), shape(TABLE, BF16), *messages,
         shape((8, faults))],
        [(TABLE, F32), ((3 * PTS + 8, FACES * E), F32), (TRACE, F32), ((MODES, WIDE), F32), (FIELD, F32)]
        + work + [(TABLE, F32)],
    )(wavefield, late, vol, part, near, own, *got, nbr_mats, face_source, fault_faces, owner, params, star,
      ap, at, al, send_faces, cluster, yield_stress, plastic_mask)
    got = exchange((m0, m1, m2, m3))
    vol, part, near = call(
        near_second_kernel, [shape(FIELD), shape(TRACE), shape(TABLE)], work[1:]
    )(integral, star, own_mats, own, high, low, face_source, av)
    nbr, delta, back = call(
        fault_kernel,
        [shape(TABLE), shape((2 * PTS, FACES * E)), shape((gy_size, 8))],
        [((3 * PTS + 8, FACES * E), F32)],
    )(near, own, *got, face_source, fault_faces, owner, params, par)
    back = lax.all_to_all(back, "gy", 0, 0, tiled=True)
    out = call(last_kernel, shape(FIELD), [(TRACE, F32), ((MODES, WIDE), F32)])(
        base, vol, part, nbr, delta, nbr_mats, al, yield_stress, plastic_mask
    )
    slip_out = call(slip_kernel, shape((1, slot_count)))(back)
    return (out, slip_out.reshape(slot_count))


def solution(mesh):
    flat = ("gx", "gy")
    last2, last3, last1 = P(None, None, flat), P(None, None, None, flat), P(flat)
    return jax.shard_map(
        local,
        mesh=mesh,
        in_specs=(
            last2, last3, last3, last3, P(), P(), P(), last1, last1, last1,
            P(None, flat), P(flat, None), P(flat, None), P(flat, None), last1, last1, last1,
        ),
        out_specs=(last2, last1),
        check_vma=False,
    )
```

```python
import jax
import jax.numpy as jnp
from jax import lax
from jax.experimental import pallas as pl
from jax.experimental.pallas import tpu as pltpu
from jax.sharding import PartitionSpec as P


F32 = jnp.float32
BF16 = jnp.bfloat16

VARS = 9
MODES = 56
FACE_PTS = 21
ORDER = 6
FACES = 4
E = 128
SLOTS = 32
PTS = 24
ROWS = 224
MSG = ROWS // 4
LIMIT = 16 * 1024 * 1024
WIDE = VARS * E


def halves(x):
    top = x.astype(BF16)
    return top, (x - top.astype(F32)).astype(BF16)


def dot(a, b):
    return jnp.dot(a, b, preferred_element_type=F32)


def iota(shape, dim):
    return lax.broadcasted_iota(jnp.int32, shape, dim)


def one_hot(mask):
    return jnp.where(mask, 1.0, 0.0).astype(BF16)


def lanes(w):
    return slice(E * w, E * (w + 1))


def widen(x):
    top = x.astype(BF16).astype(F32)
    rest = x - top
    pair = [part + pltpu.roll(part, 64, 1) for part in (top, rest)]
    return jnp.concatenate(pair, axis=1).astype(BF16)


def stack_stiffness(stiff_ref, tall_ref):
    tall_ref[...] = jnp.zeros_like(tall_ref)
    for d in range(3):
        tall_ref[MODES * d : MODES * (d + 1), 0:MODES] = -stiff_ref[d]
    return widen(tall_ref[...])


def stack_stiffness_t(stiff_ref, tall_ref, square_ref):
    square_ref[...] = jnp.zeros_like(square_ref)
    for d in range(3):
        square_ref[0:MODES, 0:MODES] = stiff_ref[d]
        tall_ref[MODES * d : MODES * (d + 1), :] = jnp.transpose(square_ref[...])[0:MODES]
    return widen(tall_ref[...])


def spread_faces(face_ref, square_ref):
    square_ref[...] = jnp.zeros_like(square_ref)
    for f in range(FACES):
        for j in range(FACE_PTS):
            square_ref[PTS * f + j : PTS * f + j + 1, 0:MODES] = face_ref[j, f : f + 1, :]


PAIRS = ((0, 1), (2, 3), (4, 5), (6, 7), (8,))


def right_operand(fields):
    pad = jnp.zeros((64 - MODES, E), F32)
    columns = []
    for x in fields:
        top = x.astype(BF16).astype(F32)
        high = jnp.concatenate([top, pad], axis=0).astype(BF16)
        low = jnp.concatenate([x - top, pad], axis=0).astype(BF16)
        columns.append(jnp.concatenate([high, low, high, low], axis=0))
    return jnp.concatenate(columns, axis=1)


def product_of(left, read, out_ref):
    for pair in PAIRS:
        cols = slice(E * pair[0], E * (pair[-1] + 1))
        out_ref[:, cols] = dot(left, right_operand([read(w) for w in pair]))


def star_mix(star_ref, tall_ref, pair):
    sums = [None] * len(pair)
    for w in range(VARS):
        for d in range(3):
            x = tall_ref[MODES * d : MODES * (d + 1), lanes(w)]
            for i, v in enumerate(pair):
                term = star_ref[v, w, d : d + 1, :] * x
                sums[i] = term if sums[i] is None else sums[i] + term
    return sums


def predict(start_ref, star_ref, left, tall_refs, early_ref, late_ref):
    product_of(left, lambda w: start_ref[w], tall_refs[0])
    factor = 1.0
    for power in range(2, ORDER + 1):
        factor = factor * power
        source, target = tall_refs[power % 2], tall_refs[(power + 1) % 2]
        for pair in PAIRS:
            derivs = star_mix(star_ref, source, pair)
            for v, deriv in zip(pair, derivs):
                for out_ref, scale in ((early_ref, 1.0 / factor), (late_ref, (2.0**power - 1.0) / factor)):
                    if out_ref is not None:
                        base = start_ref[v] if power == 2 else out_ref[v]
                        out_ref[v] = base + deriv * scale
            if power < ORDER:
                cols = slice(E * pair[0], E * (pair[-1] + 1))
                target[:, cols] = dot(left, right_operand(derivs))


def direction_rows(send_ref):
    rows = [send_ref[d : d + 1, :] for d in range(4)]
    order = []
    for axis, base in (("gx", 0), ("gy", 2)):
        odd = lax.axis_index(axis) % 2 == 1
        order.append(jnp.where(odd, rows[base], rows[base + 1]))
        order.append(jnp.where(odd, rows[base + 1], rows[base]))
    return order


def make_traces(left, integral_ref, own_ref, table_ref, high_ref, low_ref):
    product_of(left, lambda w: integral_ref[w], own_ref)
    for w in range(VARS):
        for f in range(FACES):
            table_ref[PTS * w : PTS * (w + 1), lanes(f)] = own_ref[PTS * f : PTS * (f + 1), lanes(w)]
    table_ref[PTS * VARS : ROWS, :] = jnp.zeros((ROWS - PTS * VARS, FACES * E), F32)
    high, low = halves(table_ref[...])
    high_ref[...] = high
    low_ref[...] = low


def make_messages(send_ref, high_ref, low_ref, out_refs):
    listed = jnp.concatenate(direction_rows(send_ref), axis=1)
    pick = one_hot(iota((FACES * E, 4 * SLOTS), 0) == listed)
    picked = dot(high_ref[...], pick) + dot(low_ref[...], pick)
    turned = [picked] + [pltpu.roll(picked, SLOTS * k, 1) for k in range(1, 4)]
    part = iota((MSG, E), 1) // SLOTS
    for b in range(4):
        packed = turned[(0 - b) % 4][0:MSG]
        for q in range(1, 4):
            packed = jnp.where(part == q, turned[(q - b) % 4][MSG * q : MSG * (q + 1)], packed)
        out_refs[b][...] = packed


def unpack_messages(in_refs):
    part = iota((MSG, E), 1) // SLOTS
    blocks = []
    for q in range(4):
        block = None
        for b in range(4):
            shift = (SLOTS * (b - q)) % E
            x = in_refs[b][...]
            x = pltpu.roll(x, shift, 1) if shift else x
            block = x if block is None else jnp.where(part == b, x, block)
        blocks.append(block)
    return jnp.concatenate(blocks, axis=0)


def received_slots(source_ref):
    slot = source_ref[...] - FACES * E
    swap_x = SLOTS * (1 - lax.axis_index("gx") % 2)
    swap_y = SLOTS * (1 - lax.axis_index("gy") % 2)
    swap = jnp.where(slot < 2 * SLOTS, swap_x, swap_y)
    return jnp.where(slot < 0, slot, slot ^ swap)


def finish_gather(source_ref, message_refs, near_ref, nbr_ref):
    slots = received_slots(source_ref)
    high, low = halves(unpack_messages(message_refs))
    for f in range(FACES):
        pick = one_hot(iota((4 * SLOTS, E), 0) == slots[f : f + 1])
        far = dot(high, pick) + dot(low, pick)
        nbr_ref[:, lanes(f)] = near_ref[:, lanes(f)] + far


def face_state(own_ref, nbr_ref, faces_row, state_ref):
    for c, (t, s) in enumerate(((0, 6), (3, 7), (5, 8))):
        for f in range(FACES):
            own_t = own_ref[PTS * f : PTS * (f + 1), lanes(t)]
            own_v = own_ref[PTS * f : PTS * (f + 1), lanes(s)]
            nbr_t = nbr_ref[PTS * t : PTS * (t + 1), lanes(f)]
            nbr_v = nbr_ref[PTS * s : PTS * (s + 1), lanes(f)]
            state_ref[PTS * c : PTS * (c + 1), lanes(f)] = 0.5 * (own_t + nbr_t) + 0.5 * (nbr_v - own_v)
    high, low = halves(state_ref[...])
    pick = one_hot(iota((FACES * E, faces_row.shape[1]), 0) == faces_row)
    return dot(high, pick) + dot(low, pick)


def column_of(row):
    count = row.shape[1]
    diagonal = iota((count, count), 0) == iota((count, count), 1)
    return jnp.sum(jnp.where(diagonal, row.astype(F32), 0.0), axis=1, keepdims=True)


def owner_masks(owner_row, gy_size):
    count = owner_row.shape[1]
    owner_col = column_of(owner_row)
    same = owner_col == owner_row.astype(F32)
    earlier = iota((count, count), 0) < iota((count, count), 1)
    rank = jnp.sum(jnp.where(same & earlier, 1.0, 0.0), axis=0, keepdims=True)
    named = iota((gy_size, count), 0) == owner_row
    return named, rank


def slot_values(params_ref, named, rank):
    out = []
    for c in range(3):
        both = []
        for r in range(2):
            col = params_ref[:, 3 * r + c : 3 * r + c + 1]
            both.append(jnp.sum(jnp.where(named, col, 0.0), axis=0, keepdims=True))
        out.append(jnp.where(rank > 0.5, both[1], both[0]))
    return out


def friction(state, slip, cohesion, flag):
    coeff = 0.6 - 0.3 * jnp.minimum(slip / 0.5, 1.0)
    normal, first, second = (state[PTS * c : PTS * (c + 1)] for c in range(3))
    strength = cohesion + coeff * jnp.maximum(-normal, 0.0)
    magnitude = jnp.sqrt(first * first + second * second)
    ratio = jnp.where(flag > 0.5, strength / jnp.maximum(magnitude, strength), 1.0)
    change = jnp.concatenate([first * (ratio - 1.0), second * (ratio - 1.0)], axis=0)
    slip_new = slip + jnp.sum(magnitude * (1.0 - ratio), axis=0, keepdims=True) / FACE_PTS
    return change, slip_new


def spread_change(change, faces_row):
    count = faces_row.shape[1]
    faces_col = column_of(faces_row)
    place = one_hot(iota((count, FACES * E), 1).astype(F32) == faces_col)
    high, low = halves(change)
    return dot(high, place) + dot(low, place)


def mix_faces(mats_ref, trace, start, flux_ref):
    def body(v, carry):
        cols = pl.ds(pl.multiple_of(v * E, E), E)
        for f in range(FACES):
            rows = slice(PTS * f, PTS * (f + 1))
            total = None if start is None else start[rows, cols]
            for w in range(VARS):
                term = mats_ref[v, w, f : f + 1, :] * trace(f, w)
                total = term if total is None else total + term
            flux_ref[rows, cols] = total
        return carry

    lax.fori_loop(0, VARS, body, 0)


def lift(lift_ref, flux_ref, out_ref):
    top = lift_ref[0][:, 0 : FACES * PTS]
    rest = lift_ref[1][:, 0 : FACES * PTS]
    for start in range(0, WIDE, 256):
        cols = slice(start, min(start + 256, WIDE))
        high, low = halves(flux_ref[:, cols])
        out_ref[:, cols] = dot(top, high) + (dot(top, low) + dot(rest, high))


def add_change(flux_ref, delta):
    for c, v in ((0, 3), (1, 5)):
        for f in range(FACES):
            rows = slice(PTS * f, PTS * (f + 1))
            flux_ref[rows, lanes(v)] = flux_ref[rows, lanes(v)] + delta[PTS * c : PTS * (c + 1), lanes(f)]


def plastic(read, mask_row, yield_row):
    q = [read(v) for v in range(6)]
    mean = (q[0] + q[1] + q[2]) / 3.0
    dev = [x - mean for x in q[0:3]]
    dev_sq = dev[0] * dev[0] + dev[1] * dev[1] + dev[2] * dev[2]
    shear_sq = q[3] * q[3] + q[4] * q[4] + q[5] * q[5]
    second = jnp.sum(dev_sq + 2.0 * shear_sq, axis=0, keepdims=True) / (2.0 * MODES)
    equiv = jnp.sqrt(second + 1e-06)
    factor = 1.0 - mask_row.astype(F32) * 0.5 * jnp.maximum(1.0 - yield_row / equiv, 0.0)
    return [mean + factor * x for x in dev] + [factor * x for x in q[3:6]]


def params_kernel(slip_ref, cohesion_ref, flag_ref, out_ref):
    gy_size = out_ref.shape[0]
    shape = (gy_size, slip_ref.shape[1])
    cols = []
    for r in range(2):
        mine = iota(shape, 1) == 2 * iota(shape, 0) + r
        for row in (slip_ref[...], cohesion_ref[...], flag_ref[...].astype(F32)):
            cols.append(jnp.sum(jnp.where(mine, row, 0.0), axis=1, keepdims=True))
    column = iota(out_ref.shape, 1)
    out = jnp.zeros(out_ref.shape, F32)
    for i, col in enumerate(cols):
        out = jnp.where(column == i, col, out)
    out_ref[...] = out


def slip_kernel(in_ref, out_ref):
    shape = (in_ref.shape[0], out_ref.shape[1])
    out = jnp.zeros((1, shape[1]), F32)
    for r in range(2):
        mine = iota(shape, 1) == 2 * iota(shape, 0) + r
        out = out + jnp.sum(jnp.where(mine, in_ref[:, r : r + 1], 0.0), axis=0, keepdims=True)
    out_ref[...] = out


def first_kernel(
    stiff_hbm, wave_hbm, star_hbm, proj_hbm, send_hbm, source_hbm, faces_hbm, owner_hbm, cluster_hbm, yield_hbm, mask_hbm,
    send_ref, source_ref, faces_ref, owner_ref, cluster_ref, yield_ref, mask_ref, early_ref, late_ref, own_ref, high_ref, low_ref, m0, m1, m2, m3, ap_ref, at_ref,
    tall_a, tall_b, lhs_ref, square_ref, table_ref,
    stiff_ref, wave_ref, star_ref, proj_ref, *sems,
):
    sources = (stiff_hbm, wave_hbm, star_hbm, proj_hbm, send_hbm, source_hbm, faces_hbm, owner_hbm, cluster_hbm, yield_hbm, mask_hbm)
    targets = (stiff_ref, wave_ref, star_ref, proj_ref, send_ref, source_ref, faces_ref, owner_ref, cluster_ref, yield_ref, mask_ref)
    copies = [pltpu.make_async_copy(*each) for each in zip(sources, targets, sems)]
    for copy in copies:
        copy.start()
    copies[0].wait()
    ap_ref[...] = stack_stiffness(stiff_ref, lhs_ref)
    copies[3].wait()
    spread_faces(proj_ref, square_ref)
    at_ref[...] = widen(square_ref[0 : FACES * PTS])
    copies[1].wait()
    copies[2].wait()
    for copy in copies[4:]:
        copy.wait()
    predict(wave_ref, star_ref, ap_ref[...], (tall_a, tall_b), early_ref, late_ref)
    make_traces(at_ref[...], early_ref, own_ref, table_ref, high_ref, low_ref)
    make_messages(send_ref, high_ref, low_ref, (m0, m1, m2, m3))


def near_work(integral_ref, star_ref, own_mats_ref, own_ref, high_ref, low_ref, source_ref, left,
              vol_ref, flux_ref, near_ref, tall_ref):
    product_of(left, lambda w: integral_ref[w], tall_ref)
    for pair in PAIRS:
        for v, total in zip(pair, star_mix(star_ref, tall_ref, pair)):
            vol_ref[v] = total
    mix_faces(own_mats_ref, lambda f, w: own_ref[PTS * f : PTS * (f + 1), lanes(w)], None, flux_ref)
    for f in range(FACES):
        pick = one_hot(iota((FACES * E, E), 0) == source_ref[f : f + 1, :])
        near_ref[:, lanes(f)] = dot(high_ref[...], pick) + dot(low_ref[...], pick)


def near_first_kernel(
    integral_ref, star_ref, own_mats_ref, own_ref, high_ref, low_ref, source_ref, stiff_ref, lift_ref,
    vol_ref, flux_ref, near_ref, av_ref, al_ref,
    tall_ref, lhs_ref, square_ref,
):
    av_ref[...] = stack_stiffness_t(stiff_ref, lhs_ref, square_ref)
    spread_faces(lift_ref, square_ref)
    high, low = halves(jnp.transpose(square_ref[...])[0:MODES])
    al_ref[0] = high
    al_ref[1] = low
    near_work(integral_ref, star_ref, own_mats_ref, own_ref, high_ref, low_ref, source_ref, av_ref[...],
              vol_ref, flux_ref, near_ref, tall_ref)


def near_second_kernel(
    integral_ref, star_ref, own_mats_ref, own_ref, high_ref, low_ref, source_ref, av_ref,
    vol_ref, flux_ref, near_ref,
    tall_ref,
):
    near_work(integral_ref, star_ref, own_mats_ref, own_ref, high_ref, low_ref, source_ref, av_ref[...],
              vol_ref, flux_ref, near_ref, tall_ref)


def middle_kernel(
    wave_ref, late_ref, vol_ref, part_ref, near_ref, own_ref, m0, m1, m2, m3, nbr_mats_ref, source_ref,
    faces_ref, owner_ref, params_ref, star_ref, ap_ref, at_ref, al_ref, send_ref, cluster_ref, yield_ref, mask_ref,
    integral_ref, base_ref, own2_ref, high_ref, low_ref, n0, n1, n2, n3, par_ref,
    nbr_ref, state_ref, flux_ref, lifted_ref, mid_ref, tall_a, tall_b, table_ref,
):
    finish_gather(source_ref, (m0, m1, m2, m3), near_ref, nbr_ref)
    faces_row = faces_ref[...]
    state = face_state(own_ref, nbr_ref, faces_row, state_ref)
    named, rank = owner_masks(owner_ref[...], params_ref.shape[0])
    slip, cohesion, flag = slot_values(params_ref, named, rank)
    change, slip_new = friction(state, slip, cohesion, flag)
    par_ref[0:1, :] = slip_new
    par_ref[1:2, :] = cohesion
    par_ref[2:3, :] = flag
    delta = spread_change(change, faces_row)
    mix_faces(
        nbr_mats_ref, lambda f, w: nbr_ref[PTS * w : PTS * (w + 1), lanes(f)], part_ref, flux_ref
    )
    add_change(flux_ref, delta)
    lift(al_ref, flux_ref, lifted_ref)
    coarse = cluster_ref[...] == 1
    for v in range(VARS):
        increment = vol_ref[v] - lifted_ref[:, lanes(v)]
        mid_ref[v] = wave_ref[v] + increment
        base_ref[v] = jnp.where(coarse, increment, 0.0)
    stressed = plastic(lambda v: mid_ref[v], mask_ref[...], yield_ref[...])
    for v in range(VARS):
        fine = stressed[v] if v < 6 else mid_ref[v]
        midway = jnp.where(coarse, wave_ref[v], fine)
        mid_ref[v] = midway
        base_ref[v] = midway + base_ref[v]
    predict(mid_ref, star_ref, ap_ref[...], (tall_a, tall_b), integral_ref, None)
    for v in range(VARS):
        integral_ref[v] = jnp.where(coarse, late_ref[v], integral_ref[v])
    make_traces(at_ref[...], integral_ref, own2_ref, table_ref, high_ref, low_ref)
    make_messages(send_ref, high_ref, low_ref, (n0, n1, n2, n3))


def fault_kernel(
    near_ref, own_ref, m0, m1, m2, m3, source_ref, faces_ref, owner_ref, params_ref, par_ref,
    nbr_ref, delta_ref, back_ref,
    state_ref,
):
    finish_gather(source_ref, (m0, m1, m2, m3), near_ref, nbr_ref)
    faces_row = faces_ref[...]
    state = face_state(own_ref, nbr_ref, faces_row, state_ref)
    change, slip_new = friction(state, par_ref[0:1, :], par_ref[1:2, :], par_ref[2:3, :])
    delta_ref[...] = spread_change(change, faces_row)
    named, rank = owner_masks(owner_ref[...], params_ref.shape[0])
    column = iota(back_ref.shape, 1)
    out = jnp.zeros(back_ref.shape, F32)
    for r in range(2):
        here = named & ((rank > 0.5) == (r == 1))
        total = jnp.sum(jnp.where(here, slip_new, 0.0), axis=1, keepdims=True)
        used = jnp.sum(jnp.where(here, 1.0, 0.0), axis=1, keepdims=True)
        value = jnp.where(used > 0.5, total, params_ref[:, 3 * r : 3 * r + 1])
        out = jnp.where(column == r, value, out)
    back_ref[...] = out


def last_kernel(
    base_ref, vol_ref, part_ref, nbr_ref, delta_ref, nbr_mats_ref, al_ref, yield_ref, mask_ref,
    out_ref,
    flux_ref, lifted_ref,
):
    mix_faces(
        nbr_mats_ref, lambda f, w: nbr_ref[PTS * w : PTS * (w + 1), lanes(f)], part_ref, flux_ref
    )
    add_change(flux_ref, delta_ref[...])
    lift(al_ref, flux_ref, lifted_ref)
    for v in range(VARS):
        out_ref[v] = base_ref[v] + (vol_ref[v] - lifted_ref[:, lanes(v)])
    stressed = plastic(lambda v: out_ref[v], mask_ref[...], yield_ref[...])
    for v in range(6):
        out_ref[v] = stressed[v]


def shape(dims, dtype=F32):
    return jax.ShapeDtypeStruct(dims, dtype)


def call(kernel, outs, scratch=(), hbm=0):
    in_vmem = pl.BlockSpec(memory_space=pltpu.VMEM)
    in_hbm = pl.BlockSpec(memory_space=pltpu.HBM)
    many = isinstance(outs, list)

    def run(*args):
        return pl.pallas_call(
            kernel,
            out_shape=outs,
            in_specs=[in_hbm] * hbm + [in_vmem] * (len(args) - hbm),
            out_specs=[in_vmem] * len(outs) if many else in_vmem,
            scratch_shapes=[pltpu.VMEM(dims, dtype) for dims, dtype in scratch] + [pltpu.SemaphoreType.DMA] * hbm,
            compiler_params=pltpu.CompilerParams(vmem_limit_bytes=LIMIT),
        )(*args)

    return run


FIELD = (VARS, MODES, E)
TRACE = (FACES * PTS, WIDE)
TABLE = (ROWS, FACES * E)
LEFT = (3 * MODES, 256)
TALL = (3 * MODES, WIDE)


def pair_up(x, axis, odd):
    count = lax.axis_size(axis)
    if odd:
        pairs = [(i, (i + 1) % count if i % 2 else (i - 1) % count) for i in range(count)]
    else:
        pairs = [(i, i ^ 1) for i in range(count)]
    return lax.ppermute(x, axis, pairs)


EDGES = (("gx", 0), ("gx", 1), ("gy", 0), ("gy", 1))


def exchange(messages):
    received = []
    for x, (axis, odd) in zip(messages, EDGES):
        received.append(pair_up(x, axis, odd))
    return received


def local(
    wavefield,
    star_mats,
    flux_own,
    flux_nbr,
    stiffness,
    face_proj,
    lift_mats,
    cluster,
    yield_stress,
    plastic_mask,
    face_source,
    send_faces,
    fault_faces,
    fault_owner,
    fault_slip,
    cohesion,
    slip_flag,
):
    gy_size = lax.axis_size("gy")
    faults = fault_faces.shape[1]
    slot_count = fault_slip.shape[0]
    star = jnp.transpose(star_mats, (1, 2, 0, 3))
    own_mats = jnp.transpose(flux_own, (1, 2, 0, 3))
    nbr_mats = jnp.transpose(flux_nbr, (1, 2, 0, 3))
    proj = jnp.transpose(face_proj, (1, 0, 2))
    lifts = jnp.transpose(lift_mats, (2, 0, 1))
    owner = jnp.transpose(fault_owner)
    cluster, yield_stress, plastic_mask = (x.reshape(1, E) for x in (cluster, yield_stress, plastic_mask))
    slots = [x.reshape(1, slot_count) for x in (fault_slip, cohesion, slip_flag)]

    params = call(params_kernel, shape((gy_size, 8)))(*slots)
    params = lax.all_to_all(params, "gy", 0, 0, tiled=True)

    messages = [shape((MSG, E))] * 4
    small = (send_faces, face_source, fault_faces, owner, cluster, yield_stress, plastic_mask)
    firsts = [pltpu.with_memory_space_constraint(x, pltpu.HBM) for x in (stiffness, wavefield, star, proj, *small)]
    work = [(TALL, F32), (TALL, F32)]
    (send_faces, face_source, fault_faces, owner, cluster, yield_stress, plastic_mask,
     early, late, own, high, low, m0, m1, m2, m3, ap, at) = call(
        first_kernel,
        [*(shape(x.shape, x.dtype) for x in small),
         shape(FIELD), shape(FIELD), shape(TRACE), shape(TABLE, BF16), shape(TABLE, BF16), *messages,
         shape(LEFT, BF16), shape((FACES * PTS, 256), BF16)],
        work + [((3 * MODES, E), F32), ((E, E), F32), (TABLE, F32)]
        + [(x.shape, x.dtype) for x in firsts[0:4]],
        hbm=len(firsts),
    )(*firsts)
    got = exchange((m0, m1, m2, m3))
    vol, part, near, av, al = call(
        near_first_kernel,
        [shape(FIELD), shape(TRACE), shape(TABLE), shape(LEFT, BF16), shape((2, MODES, E), BF16)],
        work[1:] + [((3 * MODES, E), F32), ((E, E), F32)],
    )(early, star, own_mats, own, high, low, face_source, stiffness, lifts)
    integral, base, own, high, low, m0, m1, m2, m3, par = call(
        middle_kernel,
        [shape(FIELD), shape(FIELD), shape(TRACE), shape(TABLE, BF16), shape(TABLE, BF16), *messages,
         shape((8, faults))],
        [(TABLE, F32), ((3 * PTS + 8, FACES * E), F32), (TRACE, F32), ((MODES, WIDE), F32), (FIELD, F32)]
        + work + [(TABLE, F32)],
    )(wavefield, late, vol, part, near, own, *got, nbr_mats, face_source, fault_faces, owner, params, star,
      ap, at, al, send_faces, cluster, yield_stress, plastic_mask)
    got = exchange((m0, m1, m2, m3))
    vol, part, near = call(
        near_second_kernel, [shape(FIELD), shape(TRACE), shape(TABLE)], work[1:]
    )(integral, star, own_mats, own, high, low, face_source, av)
    nbr, delta, back = call(
        fault_kernel,
        [shape(TABLE), shape((2 * PTS, FACES * E)), shape((gy_size, 8))],
        [((3 * PTS + 8, FACES * E), F32)],
    )(near, own, *got, face_source, fault_faces, owner, params, par)
    back = lax.all_to_all(back, "gy", 0, 0, tiled=True)
    out = call(last_kernel, shape(FIELD), [(TRACE, F32), ((MODES, WIDE), F32)])(
        base, vol, part, nbr, delta, nbr_mats, al, yield_stress, plastic_mask
    )
    slip_out = call(slip_kernel, shape((1, slot_count)))(back)
    return (out, slip_out.reshape(slot_count))


def solution(mesh):
    flat = ("gx", "gy")
    last2, last3, last1 = P(None, None, flat), P(None, None, None, flat), P(flat)

    return jax.shard_map(
        local,
        mesh=mesh,
        in_specs=(
            last2, last3, last3, last3, P(), P(), P(), last1, last1, last1,
            P(None, flat), P(flat, None), P(flat, None), P(flat, None), last1, last1, last1,
        ),
        out_specs=(last2, last1),
        check_vma=False,
    )
```

```python
import jax
import jax.numpy as jnp
from jax import lax
from jax.experimental import pallas as pl
from jax.experimental.pallas import tpu as pltpu
from jax.sharding import PartitionSpec as P


F32 = jnp.float32
BF16 = jnp.bfloat16

VARS = 9
MODES = 56
FACE_PTS = 21
ORDER = 6
FACES = 4
E = 128
SLOTS = 32
PTS = 24
ROWS = 224
MSG = ROWS // 4
LIMIT = 16 * 1024 * 1024
WIDE = VARS * E


def halves(x):
    top = x.astype(BF16)
    return top, (x - top.astype(F32)).astype(BF16)


def dot(a, b):
    return jnp.dot(a, b, preferred_element_type=F32)


def iota(shape, dim):
    return lax.broadcasted_iota(jnp.int32, shape, dim)


def one_hot(mask):
    return jnp.where(mask, 1.0, 0.0).astype(BF16)


def lanes(w):
    return slice(E * w, E * (w + 1))


def widen(x):
    top = x.astype(BF16).astype(F32)
    rest = x - top
    pair = [part + pltpu.roll(part, 64, 1) for part in (top, rest)]
    return jnp.concatenate(pair, axis=1).astype(BF16)


def stack_stiffness(stiff_ref, tall_ref):
    tall_ref[...] = jnp.zeros_like(tall_ref)
    for d in range(3):
        tall_ref[MODES * d : MODES * (d + 1), 0:MODES] = -stiff_ref[d]
    return widen(tall_ref[...])


def stack_stiffness_t(stiff_ref, tall_ref, square_ref):
    square_ref[...] = jnp.zeros_like(square_ref)
    for d in range(3):
        square_ref[0:MODES, 0:MODES] = stiff_ref[d]
        tall_ref[MODES * d : MODES * (d + 1), :] = jnp.transpose(square_ref[...])[0:MODES]
    return widen(tall_ref[...])


def spread_faces(face_ref, square_ref):
    square_ref[...] = jnp.zeros_like(square_ref)
    for f in range(FACES):
        for j in range(FACE_PTS):
            square_ref[PTS * f + j : PTS * f + j + 1, 0:MODES] = face_ref[j, f : f + 1, :]


PAIRS = ((0, 1), (2, 3), (4, 5), (6, 7), (8,))


def right_operand(fields):
    pad = jnp.zeros((64 - MODES, E), F32)
    columns = []
    for x in fields:
        top = x.astype(BF16).astype(F32)
        high = jnp.concatenate([top, pad], axis=0).astype(BF16)
        low = jnp.concatenate([x - top, pad], axis=0).astype(BF16)
        columns.append(jnp.concatenate([high, low, high, low], axis=0))
    return jnp.concatenate(columns, axis=1)


def product_of(left, read, out_ref):
    for pair in PAIRS:
        cols = slice(E * pair[0], E * (pair[-1] + 1))
        out_ref[:, cols] = dot(left, right_operand([read(w) for w in pair]))


def star_mix(star_ref, tall_ref, pair):
    sums = [None] * len(pair)
    for w in range(VARS):
        for d in range(3):
            x = tall_ref[MODES * d : MODES * (d + 1), lanes(w)]
            for i, v in enumerate(pair):
                term = star_ref[v, w, d : d + 1, :] * x
                sums[i] = term if sums[i] is None else sums[i] + term
    return sums


def predict(start_ref, star_ref, left, tall_refs, early_ref, late_ref):
    product_of(left, lambda w: start_ref[w], tall_refs[0])
    factor = 1.0
    for power in range(2, ORDER + 1):
        factor = factor * power
        source, target = tall_refs[power % 2], tall_refs[(power + 1) % 2]
        for pair in PAIRS:
            derivs = star_mix(star_ref, source, pair)
            for v, deriv in zip(pair, derivs):
                for out_ref, scale in ((early_ref, 1.0 / factor), (late_ref, (2.0**power - 1.0) / factor)):
                    if out_ref is not None:
                        base = start_ref[v] if power == 2 else out_ref[v]
                        out_ref[v] = base + deriv * scale
            if power < ORDER:
                cols = slice(E * pair[0], E * (pair[-1] + 1))
                target[:, cols] = dot(left, right_operand(derivs))


def direction_rows(send_ref):
    rows = [send_ref[d : d + 1, :] for d in range(4)]
    order = []
    for axis, base in (("gx", 0), ("gy", 2)):
        odd = lax.axis_index(axis) % 2 == 1
        order.append(jnp.where(odd, rows[base], rows[base + 1]))
        order.append(jnp.where(odd, rows[base + 1], rows[base]))
    return order


def make_traces(left, integral_ref, own_ref, table_ref, high_ref, low_ref):
    product_of(left, lambda w: integral_ref[w], own_ref)
    for w in range(VARS):
        for f in range(FACES):
            table_ref[PTS * w : PTS * (w + 1), lanes(f)] = own_ref[PTS * f : PTS * (f + 1), lanes(w)]
    table_ref[PTS * VARS : ROWS, :] = jnp.zeros((ROWS - PTS * VARS, FACES * E), F32)
    high, low = halves(table_ref[...])
    high_ref[...] = high
    low_ref[...] = low


def make_messages(send_ref, high_ref, low_ref, out_refs):
    listed = jnp.concatenate(direction_rows(send_ref), axis=1)
    pick = one_hot(iota((FACES * E, 4 * SLOTS), 0) == listed)
    picked = dot(high_ref[...], pick) + dot(low_ref[...], pick)
    turned = [picked] + [pltpu.roll(picked, SLOTS * k, 1) for k in range(1, 4)]
    part = iota((MSG, E), 1) // SLOTS
    for b in range(4):
        packed = turned[(0 - b) % 4][0:MSG]
        for q in range(1, 4):
            packed = jnp.where(part == q, turned[(q - b) % 4][MSG * q : MSG * (q + 1)], packed)
        out_refs[b][...] = packed


def unpack_messages(in_refs):
    part = iota((MSG, E), 1) // SLOTS
    blocks = []
    for q in range(4):
        block = None
        for b in range(4):
            shift = (SLOTS * (b - q)) % E
            x = in_refs[b][...]
            x = pltpu.roll(x, shift, 1) if shift else x
            block = x if block is None else jnp.where(part == b, x, block)
        blocks.append(block)
    return jnp.concatenate(blocks, axis=0)


def received_slots(source_ref):
    slot = source_ref[...] - FACES * E
    swap_x = SLOTS * (1 - lax.axis_index("gx") % 2)
    swap_y = SLOTS * (1 - lax.axis_index("gy") % 2)
    swap = jnp.where(slot < 2 * SLOTS, swap_x, swap_y)
    return jnp.where(slot < 0, slot, slot ^ swap)


def finish_gather(source_ref, message_refs, near_ref, nbr_ref):
    slots = received_slots(source_ref)
    high, low = halves(unpack_messages(message_refs))
    for f in range(FACES):
        pick = one_hot(iota((4 * SLOTS, E), 0) == slots[f : f + 1])
        far = dot(high, pick) + dot(low, pick)
        nbr_ref[:, lanes(f)] = near_ref[:, lanes(f)] + far


def face_state(own_ref, nbr_ref, faces_row, state_ref):
    for c, (t, s) in enumerate(((0, 6), (3, 7), (5, 8))):
        for f in range(FACES):
            own_t = own_ref[PTS * f : PTS * (f + 1), lanes(t)]
            own_v = own_ref[PTS * f : PTS * (f + 1), lanes(s)]
            nbr_t = nbr_ref[PTS * t : PTS * (t + 1), lanes(f)]
            nbr_v = nbr_ref[PTS * s : PTS * (s + 1), lanes(f)]
            state_ref[PTS * c : PTS * (c + 1), lanes(f)] = 0.5 * (own_t + nbr_t) + 0.5 * (nbr_v - own_v)
    high, low = halves(state_ref[...])
    pick = one_hot(iota((FACES * E, faces_row.shape[1]), 0) == faces_row)
    return dot(high, pick) + dot(low, pick)


def column_of(row):
    count = row.shape[1]
    diagonal = iota((count, count), 0) == iota((count, count), 1)
    return jnp.sum(jnp.where(diagonal, row.astype(F32), 0.0), axis=1, keepdims=True)


def owner_masks(owner_row, gy_size):
    count = owner_row.shape[1]
    owner_col = column_of(owner_row)
    same = owner_col == owner_row.astype(F32)
    earlier = iota((count, count), 0) < iota((count, count), 1)
    rank = jnp.sum(jnp.where(same & earlier, 1.0, 0.0), axis=0, keepdims=True)
    named = iota((gy_size, count), 0) == owner_row
    return named, rank


def slot_values(params_ref, named, rank):
    out = []
    for c in range(3):
        both = []
        for r in range(2):
            col = params_ref[:, 3 * r + c : 3 * r + c + 1]
            both.append(jnp.sum(jnp.where(named, col, 0.0), axis=0, keepdims=True))
        out.append(jnp.where(rank > 0.5, both[1], both[0]))
    return out


def friction(state, slip, cohesion, flag):
    coeff = 0.6 - 0.3 * jnp.minimum(slip / 0.5, 1.0)
    normal, first, second = (state[PTS * c : PTS * (c + 1)] for c in range(3))
    strength = cohesion + coeff * jnp.maximum(-normal, 0.0)
    magnitude = jnp.sqrt(first * first + second * second)
    ratio = jnp.where(flag > 0.5, strength / jnp.maximum(magnitude, strength), 1.0)
    change = jnp.concatenate([first * (ratio - 1.0), second * (ratio - 1.0)], axis=0)
    slip_new = slip + jnp.sum(magnitude * (1.0 - ratio), axis=0, keepdims=True) / FACE_PTS
    return change, slip_new


def spread_change(change, faces_row):
    count = faces_row.shape[1]
    faces_col = column_of(faces_row)
    place = one_hot(iota((count, FACES * E), 1).astype(F32) == faces_col)
    high, low = halves(change)
    return dot(high, place) + dot(low, place)


def mix_faces(mats_ref, trace, start, flux_ref):
    def body(v, carry):
        cols = pl.ds(pl.multiple_of(v * E, E), E)
        for f in range(FACES):
            rows = slice(PTS * f, PTS * (f + 1))
            total = None if start is None else start[rows, cols]
            for w in range(VARS):
                term = mats_ref[v, w, f : f + 1, :] * trace(f, w)
                total = term if total is None else total + term
            flux_ref[rows, cols] = total
        return carry

    lax.fori_loop(0, VARS, body, 0)


def lift(lift_ref, flux_ref, out_ref):
    top = lift_ref[0][:, 0 : FACES * PTS]
    rest = lift_ref[1][:, 0 : FACES * PTS]
    for start in range(0, WIDE, 256):
        cols = slice(start, min(start + 256, WIDE))
        high, low = halves(flux_ref[:, cols])
        out_ref[:, cols] = dot(top, high) + (dot(top, low) + dot(rest, high))


def add_change(flux_ref, delta):
    for c, v in ((0, 3), (1, 5)):
        for f in range(FACES):
            rows = slice(PTS * f, PTS * (f + 1))
            flux_ref[rows, lanes(v)] = flux_ref[rows, lanes(v)] + delta[PTS * c : PTS * (c + 1), lanes(f)]


def plastic(read, mask_row, yield_row):
    q = [read(v) for v in range(6)]
    mean = (q[0] + q[1] + q[2]) / 3.0
    dev = [x - mean for x in q[0:3]]
    dev_sq = dev[0] * dev[0] + dev[1] * dev[1] + dev[2] * dev[2]
    shear_sq = q[3] * q[3] + q[4] * q[4] + q[5] * q[5]
    second = jnp.sum(dev_sq + 2.0 * shear_sq, axis=0, keepdims=True) / (2.0 * MODES)
    equiv = jnp.sqrt(second + 1e-06)
    factor = 1.0 - mask_row.astype(F32) * 0.5 * jnp.maximum(1.0 - yield_row / equiv, 0.0)
    return [mean + factor * x for x in dev] + [factor * x for x in q[3:6]]


def params_kernel(count, *refs):
    inputs, out_ref, passed = refs[0 : 3 + count], refs[3 + count], refs[4 + count : 4 + 2 * count]
    slots, sems = refs[4 + 2 * count : 7 + 2 * count], refs[7 + 2 * count :]
    copies = [pltpu.make_async_copy(*each) for each in zip(inputs, (*slots, *passed), sems)]
    for copy in copies:
        copy.start()
    for copy in copies[0:3]:
        copy.wait()
    slip_ref, cohesion_ref, flag_ref = slots
    gy_size = out_ref.shape[0]
    shape = (gy_size, slip_ref.shape[1])
    cols = []
    for r in range(2):
        mine = iota(shape, 1) == 2 * iota(shape, 0) + r
        for row in (slip_ref[...], cohesion_ref[...], flag_ref[...].astype(F32)):
            cols.append(jnp.sum(jnp.where(mine, row, 0.0), axis=1, keepdims=True))
    column = iota(out_ref.shape, 1)
    out = jnp.zeros(out_ref.shape, F32)
    for i, col in enumerate(cols):
        out = jnp.where(column == i, col, out)
    out_ref[...] = out
    for copy in copies[3:]:
        copy.wait()


def slip_kernel(in_ref, out_ref):
    shape = (in_ref.shape[0], out_ref.shape[1])
    out = jnp.zeros((1, shape[1]), F32)
    for r in range(2):
        mine = iota(shape, 1) == 2 * iota(shape, 0) + r
        out = out + jnp.sum(jnp.where(mine, in_ref[:, r : r + 1], 0.0), axis=0, keepdims=True)
    out_ref[...] = out


def first_kernel(
    stiff_ref, wave_ref, star_ref, proj_ref, send_ref,
    early_ref, late_ref, own_ref, high_ref, low_ref, m0, m1, m2, m3, ap_ref, at_ref,
    tall_a, tall_b, lhs_ref, square_ref, table_ref,
):
    ap_ref[...] = stack_stiffness(stiff_ref, lhs_ref)
    spread_faces(proj_ref, square_ref)
    at_ref[...] = widen(square_ref[0 : FACES * PTS])
    predict(wave_ref, star_ref, ap_ref[...], (tall_a, tall_b), early_ref, late_ref)
    make_traces(at_ref[...], early_ref, own_ref, table_ref, high_ref, low_ref)
    make_messages(send_ref, high_ref, low_ref, (m0, m1, m2, m3))


def near_work(integral_ref, star_ref, own_mats_ref, own_ref, high_ref, low_ref, source_ref, left,
              vol_ref, flux_ref, near_ref, tall_ref):
    product_of(left, lambda w: integral_ref[w], tall_ref)
    for pair in PAIRS:
        for v, total in zip(pair, star_mix(star_ref, tall_ref, pair)):
            vol_ref[v] = total
    mix_faces(own_mats_ref, lambda f, w: own_ref[PTS * f : PTS * (f + 1), lanes(w)], None, flux_ref)
    for f in range(FACES):
        pick = one_hot(iota((FACES * E, E), 0) == source_ref[f : f + 1, :])
        near_ref[:, lanes(f)] = dot(high_ref[...], pick) + dot(low_ref[...], pick)


def near_first_kernel(
    integral_ref, star_ref, own_mats_ref, own_ref, high_ref, low_ref, source_ref, stiff_ref, lift_ref,
    vol_ref, flux_ref, near_ref, av_ref, al_ref,
    tall_ref, lhs_ref, square_ref,
):
    av_ref[...] = stack_stiffness_t(stiff_ref, lhs_ref, square_ref)
    spread_faces(lift_ref, square_ref)
    high, low = halves(jnp.transpose(square_ref[...])[0:MODES])
    al_ref[0] = high
    al_ref[1] = low
    near_work(integral_ref, star_ref, own_mats_ref, own_ref, high_ref, low_ref, source_ref, av_ref[...],
              vol_ref, flux_ref, near_ref, tall_ref)


def near_second_kernel(
    integral_ref, star_ref, own_mats_ref, own_ref, high_ref, low_ref, source_ref, av_ref,
    vol_ref, flux_ref, near_ref,
    tall_ref,
):
    near_work(integral_ref, star_ref, own_mats_ref, own_ref, high_ref, low_ref, source_ref, av_ref[...],
              vol_ref, flux_ref, near_ref, tall_ref)


def middle_kernel(
    wave_ref, late_ref, vol_ref, part_ref, near_ref, own_ref, m0, m1, m2, m3, nbr_mats_ref, source_ref,
    faces_ref, owner_ref, params_ref, star_ref, ap_ref, at_ref, al_ref, send_ref, cluster_ref, yield_ref, mask_ref,
    integral_ref, base_ref, own2_ref, high_ref, low_ref, n0, n1, n2, n3, par_ref,
    nbr_ref, state_ref, flux_ref, lifted_ref, mid_ref, tall_a, tall_b, table_ref,
):
    finish_gather(source_ref, (m0, m1, m2, m3), near_ref, nbr_ref)
    faces_row = faces_ref[...]
    state = face_state(own_ref, nbr_ref, faces_row, state_ref)
    named, rank = owner_masks(owner_ref[...], params_ref.shape[0])
    slip, cohesion, flag = slot_values(params_ref, named, rank)
    change, slip_new = friction(state, slip, cohesion, flag)
    par_ref[0:1, :] = slip_new
    par_ref[1:2, :] = cohesion
    par_ref[2:3, :] = flag
    delta = spread_change(change, faces_row)
    mix_faces(
        nbr_mats_ref, lambda f, w: nbr_ref[PTS * w : PTS * (w + 1), lanes(f)], part_ref, flux_ref
    )
    add_change(flux_ref, delta)
    lift(al_ref, flux_ref, lifted_ref)
    coarse = cluster_ref[...] == 1
    for v in range(VARS):
        increment = vol_ref[v] - lifted_ref[:, lanes(v)]
        mid_ref[v] = wave_ref[v] + increment
        base_ref[v] = jnp.where(coarse, increment, 0.0)
    stressed = plastic(lambda v: mid_ref[v], mask_ref[...], yield_ref[...])
    for v in range(VARS):
        fine = stressed[v] if v < 6 else mid_ref[v]
        midway = jnp.where(coarse, wave_ref[v], fine)
        mid_ref[v] = midway
        base_ref[v] = midway + base_ref[v]
    predict(mid_ref, star_ref, ap_ref[...], (tall_a, tall_b), integral_ref, None)
    for v in range(VARS):
        integral_ref[v] = jnp.where(coarse, late_ref[v], integral_ref[v])
    make_traces(at_ref[...], integral_ref, own2_ref, table_ref, high_ref, low_ref)
    make_messages(send_ref, high_ref, low_ref, (n0, n1, n2, n3))


def fault_kernel(
    near_ref, own_ref, m0, m1, m2, m3, source_ref, faces_ref, owner_ref, params_ref, par_ref,
    nbr_ref, delta_ref, back_ref,
    state_ref,
):
    finish_gather(source_ref, (m0, m1, m2, m3), near_ref, nbr_ref)
    faces_row = faces_ref[...]
    state = face_state(own_ref, nbr_ref, faces_row, state_ref)
    change, slip_new = friction(state, par_ref[0:1, :], par_ref[1:2, :], par_ref[2:3, :])
    delta_ref[...] = spread_change(change, faces_row)
    named, rank = owner_masks(owner_ref[...], params_ref.shape[0])
    column = iota(back_ref.shape, 1)
    out = jnp.zeros(back_ref.shape, F32)
    for r in range(2):
        here = named & ((rank > 0.5) == (r == 1))
        total = jnp.sum(jnp.where(here, slip_new, 0.0), axis=1, keepdims=True)
        used = jnp.sum(jnp.where(here, 1.0, 0.0), axis=1, keepdims=True)
        value = jnp.where(used > 0.5, total, params_ref[:, 3 * r : 3 * r + 1])
        out = jnp.where(column == r, value, out)
    back_ref[...] = out


def last_kernel(
    base_ref, vol_ref, part_ref, nbr_ref, delta_ref, nbr_mats_ref, al_ref, yield_ref, mask_ref,
    out_ref,
    flux_ref, lifted_ref,
):
    mix_faces(
        nbr_mats_ref, lambda f, w: nbr_ref[PTS * w : PTS * (w + 1), lanes(f)], part_ref, flux_ref
    )
    add_change(flux_ref, delta_ref[...])
    lift(al_ref, flux_ref, lifted_ref)
    for v in range(VARS):
        out_ref[v] = base_ref[v] + (vol_ref[v] - lifted_ref[:, lanes(v)])
    stressed = plastic(lambda v: out_ref[v], mask_ref[...], yield_ref[...])
    for v in range(6):
        out_ref[v] = stressed[v]


def in_hbm(x):
    return pltpu.with_memory_space_constraint(x, pltpu.HBM)


def shape(dims, dtype=F32):
    return jax.ShapeDtypeStruct(dims, dtype)


def call(kernel, outs, scratch=(), hbm=0):
    in_vmem = pl.BlockSpec(memory_space=pltpu.VMEM)
    from_hbm = pl.BlockSpec(memory_space=pltpu.HBM)
    many = isinstance(outs, list)

    def run(*args):
        return pl.pallas_call(
            kernel,
            out_shape=outs,
            in_specs=[from_hbm] * hbm + [in_vmem] * (len(args) - hbm),
            out_specs=[in_vmem] * len(outs) if many else in_vmem,
            scratch_shapes=[pltpu.VMEM(dims, dtype) for dims, dtype in scratch] + [pltpu.SemaphoreType.DMA] * hbm,
            compiler_params=pltpu.CompilerParams(vmem_limit_bytes=LIMIT),
        )(*args)

    return run


FIELD = (VARS, MODES, E)
TRACE = (FACES * PTS, WIDE)
TABLE = (ROWS, FACES * E)
LEFT = (3 * MODES, 256)
TALL = (3 * MODES, WIDE)


def pair_up(x, axis, odd):
    count = lax.axis_size(axis)
    if odd:
        pairs = [(i, (i + 1) % count if i % 2 else (i - 1) % count) for i in range(count)]
    else:
        pairs = [(i, i ^ 1) for i in range(count)]
    return lax.ppermute(x, axis, pairs)


EDGES = (("gx", 0), ("gx", 1), ("gy", 0), ("gy", 1))


def exchange(messages):
    received = []
    for x, (axis, odd) in zip(messages, EDGES):
        received.append(pair_up(x, axis, odd))
    return received


def local(
    wavefield,
    star_mats,
    flux_own,
    flux_nbr,
    stiffness,
    face_proj,
    lift_mats,
    cluster,
    yield_stress,
    plastic_mask,
    face_source,
    send_faces,
    fault_faces,
    fault_owner,
    fault_slip,
    cohesion,
    slip_flag,
):
    gy_size = lax.axis_size("gy")
    faults = fault_faces.shape[1]
    slot_count = fault_slip.shape[0]
    star = jnp.transpose(star_mats, (1, 2, 0, 3))
    own_mats = jnp.transpose(flux_own, (1, 2, 0, 3))
    nbr_mats = jnp.transpose(flux_nbr, (1, 2, 0, 3))
    proj = jnp.transpose(face_proj, (1, 0, 2))
    lifts = jnp.transpose(lift_mats, (2, 0, 1))
    owner = jnp.transpose(fault_owner)
    cluster, yield_stress, plastic_mask = (x.reshape(1, E) for x in (cluster, yield_stress, plastic_mask))
    slots = [x.reshape(1, slot_count) for x in (fault_slip, cohesion, slip_flag)]

    small = (send_faces, face_source, fault_faces, owner, cluster, yield_stress, plastic_mask)
    firsts = (stiffness, wavefield, star, proj, *small)
    params, *brought = call(
        lambda *refs: params_kernel(len(firsts), *refs),
        [shape((gy_size, 8)), *(shape(x.shape, x.dtype) for x in firsts)],
        [(x.shape, x.dtype) for x in slots],
        hbm=3 + len(firsts),
    )(*(in_hbm(x) for x in (*slots, *firsts)))
    stiffness, wavefield, star_first, proj = brought[0:4]
    send_faces, face_source, fault_faces, owner, cluster, yield_stress, plastic_mask = brought[4:]
    params = lax.all_to_all(params, "gy", 0, 0, tiled=True)

    messages = [shape((MSG, E))] * 4
    work = [(TALL, F32), (TALL, F32)]
    early, late, own, high, low, m0, m1, m2, m3, ap, at = call(
        first_kernel,
        [shape(FIELD), shape(FIELD), shape(TRACE), shape(TABLE, BF16), shape(TABLE, BF16), *messages,
         shape(LEFT, BF16), shape((FACES * PTS, 256), BF16)],
        work + [((3 * MODES, E), F32), ((E, E), F32), (TABLE, F32)],
    )(stiffness, wavefield, star_first, proj, send_faces)
    got = exchange((m0, m1, m2, m3))
    vol, part, near, av, al = call(
        near_first_kernel,
        [shape(FIELD), shape(TRACE), shape(TABLE), shape(LEFT, BF16), shape((2, MODES, E), BF16)],
        work[1:] + [((3 * MODES, E), F32), ((E, E), F32)],
    )(early, star, own_mats, own, high, low, face_source, stiffness, lifts)
    integral, base, own, high, low, m0, m1, m2, m3, par = call(
        middle_kernel,
        [shape(FIELD), shape(FIELD), shape(TRACE), shape(TABLE, BF16), shape(TABLE, BF16), *messages,
         shape((8, faults))],
        [(TABLE, F32), ((3 * PTS + 8, FACES * E), F32), (TRACE, F32), ((MODES, WIDE), F32), (FIELD, F32)]
        + work + [(TABLE, F32)],
    )(wavefield, late, vol, part, near, own, *got, nbr_mats, face_source, fault_faces, owner, params, star,
      ap, at, al, send_faces, cluster, yield_stress, plastic_mask)
    got = exchange((m0, m1, m2, m3))
    vol, part, near = call(
        near_second_kernel, [shape(FIELD), shape(TRACE), shape(TABLE)], work[1:]
    )(integral, star, own_mats, own, high, low, face_source, av)
    nbr, delta, back = call(
        fault_kernel,
        [shape(TABLE), shape((2 * PTS, FACES * E)), shape((gy_size, 8))],
        [((3 * PTS + 8, FACES * E), F32)],
    )(near, own, *got, face_source, fault_faces, owner, params, par)
    back = lax.all_to_all(back, "gy", 0, 0, tiled=True)
    out = call(last_kernel, shape(FIELD), [(TRACE, F32), ((MODES, WIDE), F32)])(
        base, vol, part, nbr, delta, nbr_mats, al, yield_stress, plastic_mask
    )
    slip_out = call(slip_kernel, shape((1, slot_count)))(back)
    return (out, slip_out.reshape(slot_count))


def solution(mesh):
    flat = ("gx", "gy")
    last2, last3, last1 = P(None, None, flat), P(None, None, None, flat), P(flat)

    return jax.shard_map(
        local,
        mesh=mesh,
        in_specs=(
            last2, last3, last3, last3, P(), P(), P(), last1, last1, last1,
            P(None, flat), P(flat, None), P(flat, None), P(flat, None), last1, last1, last1,
        ),
        out_specs=(last2, last1),
        check_vma=False,
    )
```

```python
import jax
import jax.numpy as jnp
from jax import lax
from jax.experimental import pallas as pl
from jax.experimental.pallas import tpu as pltpu
from jax.sharding import PartitionSpec as P


F32 = jnp.float32
BF16 = jnp.bfloat16

VARS = 9
MODES = 56
FACE_PTS = 21
ORDER = 6
FACES = 4
E = 128
SLOTS = 32
PTS = 24
ROWS = 224
MSG = ROWS // 4
LIMIT = 16 * 1024 * 1024
WIDE = VARS * E


def halves(x):
    top = x.astype(BF16)
    return top, (x - top.astype(F32)).astype(BF16)


def dot(a, b):
    return jnp.dot(a, b, preferred_element_type=F32)


def iota(shape, dim):
    return lax.broadcasted_iota(jnp.int32, shape, dim)


def one_hot(mask):
    return jnp.where(mask, 1.0, 0.0).astype(BF16)


def lanes(w):
    return slice(E * w, E * (w + 1))


def widen(x):
    top = x.astype(BF16).astype(F32)
    rest = x - top
    pair = [part + pltpu.roll(part, 64, 1) for part in (top, rest)]
    return jnp.concatenate(pair, axis=1).astype(BF16)


def stack_stiffness(stiff_ref, tall_ref):
    tall_ref[...] = jnp.zeros_like(tall_ref)
    for d in range(3):
        tall_ref[MODES * d : MODES * (d + 1), 0:MODES] = -stiff_ref[d]
    return widen(tall_ref[...])


def stack_stiffness_t(stiff_ref, tall_ref, square_ref):
    square_ref[...] = jnp.zeros_like(square_ref)
    for d in range(3):
        square_ref[0:MODES, 0:MODES] = stiff_ref[d]
        tall_ref[MODES * d : MODES * (d + 1), :] = jnp.transpose(square_ref[...])[0:MODES]
    return widen(tall_ref[...])


def spread_faces(face_ref, square_ref):
    square_ref[...] = jnp.zeros_like(square_ref)
    for f in range(FACES):
        for j in range(FACE_PTS):
            square_ref[PTS * f + j : PTS * f + j + 1, 0:MODES] = face_ref[j, f : f + 1, :]


PAIRS = ((0, 1), (2, 3), (4, 5), (6, 7), (8,))


def right_operand(fields):
    pad = jnp.zeros((64 - MODES, E), F32)
    columns = []
    for x in fields:
        top = x.astype(BF16).astype(F32)
        high = jnp.concatenate([top, pad], axis=0).astype(BF16)
        low = jnp.concatenate([x - top, pad], axis=0).astype(BF16)
        columns.append(jnp.concatenate([high, low, high, low], axis=0))
    return jnp.concatenate(columns, axis=1)


def product_of(left, read, out_ref):
    for pair in PAIRS:
        cols = slice(E * pair[0], E * (pair[-1] + 1))
        out_ref[:, cols] = dot(left, right_operand([read(w) for w in pair]))


def star_mix(star_ref, tall_ref, pair):
    sums = [None] * len(pair)
    for w in range(VARS):
        for d in range(3):
            x = tall_ref[MODES * d : MODES * (d + 1), lanes(w)]
            for i, v in enumerate(pair):
                term = star_ref[v, w, d : d + 1, :] * x
                sums[i] = term if sums[i] is None else sums[i] + term
    return sums


def predict(start_ref, star_ref, left, tall_refs, early_ref, late_ref):
    product_of(left, lambda w: start_ref[w], tall_refs[0])
    factor = 1.0
    for power in range(2, ORDER + 1):
        factor = factor * power
        source, target = tall_refs[power % 2], tall_refs[(power + 1) % 2]
        for pair in PAIRS:
            derivs = star_mix(star_ref, source, pair)
            for v, deriv in zip(pair, derivs):
                for out_ref, scale in ((early_ref, 1.0 / factor), (late_ref, (2.0**power - 1.0) / factor)):
                    if out_ref is not None:
                        base = start_ref[v] if power == 2 else out_ref[v]
                        out_ref[v] = base + deriv * scale
            if power < ORDER:
                cols = slice(E * pair[0], E * (pair[-1] + 1))
                target[:, cols] = dot(left, right_operand(derivs))


def direction_rows(send_ref):
    rows = [send_ref[d : d + 1, :] for d in range(4)]
    order = []
    for axis, base in (("gx", 0), ("gy", 2)):
        odd = lax.axis_index(axis) % 2 == 1
        order.append(jnp.where(odd, rows[base], rows[base + 1]))
        order.append(jnp.where(odd, rows[base + 1], rows[base]))
    return order


def make_traces(left, integral_ref, own_ref, table_ref, high_ref, low_ref):
    product_of(left, lambda w: integral_ref[w], own_ref)
    for w in range(VARS):
        for f in range(FACES):
            table_ref[PTS * w : PTS * (w + 1), lanes(f)] = own_ref[PTS * f : PTS * (f + 1), lanes(w)]
    table_ref[PTS * VARS : ROWS, :] = jnp.zeros((ROWS - PTS * VARS, FACES * E), F32)
    high, low = halves(table_ref[...])
    high_ref[...] = high
    low_ref[...] = low


def make_messages(send_ref, high_ref, low_ref, out_refs):
    listed = jnp.concatenate(direction_rows(send_ref), axis=1)
    pick = one_hot(iota((FACES * E, 4 * SLOTS), 0) == listed)
    picked = dot(high_ref[...], pick) + dot(low_ref[...], pick)
    turned = [picked] + [pltpu.roll(picked, SLOTS * k, 1) for k in range(1, 4)]
    part = iota((MSG, E), 1) // SLOTS
    for b in range(4):
        packed = turned[(0 - b) % 4][0:MSG]
        for q in range(1, 4):
            packed = jnp.where(part == q, turned[(q - b) % 4][MSG * q : MSG * (q + 1)], packed)
        out_refs[b][...] = packed


def unpack_messages(in_refs):
    part = iota((MSG, E), 1) // SLOTS
    blocks = []
    for q in range(4):
        block = None
        for b in range(4):
            shift = (SLOTS * (b - q)) % E
            x = in_refs[b][...]
            x = pltpu.roll(x, shift, 1) if shift else x
            block = x if block is None else jnp.where(part == b, x, block)
        blocks.append(block)
    return jnp.concatenate(blocks, axis=0)


def received_slots(source_ref):
    slot = source_ref[...] - FACES * E
    swap_x = SLOTS * (1 - lax.axis_index("gx") % 2)
    swap_y = SLOTS * (1 - lax.axis_index("gy") % 2)
    swap = jnp.where(slot < 2 * SLOTS, swap_x, swap_y)
    return jnp.where(slot < 0, slot, slot ^ swap)


def finish_gather(source_ref, message_refs, near_ref, nbr_ref):
    slots = received_slots(source_ref)
    high, low = halves(unpack_messages(message_refs))
    for f in range(FACES):
        pick = one_hot(iota((4 * SLOTS, E), 0) == slots[f : f + 1])
        far = dot(high, pick) + dot(low, pick)
        nbr_ref[:, lanes(f)] = near_ref[:, lanes(f)] + far


def face_state(own_ref, nbr_ref, faces_row, state_ref):
    for c, (t, s) in enumerate(((0, 6), (3, 7), (5, 8))):
        for f in range(FACES):
            own_t = own_ref[PTS * f : PTS * (f + 1), lanes(t)]
            own_v = own_ref[PTS * f : PTS * (f + 1), lanes(s)]
            nbr_t = nbr_ref[PTS * t : PTS * (t + 1), lanes(f)]
            nbr_v = nbr_ref[PTS * s : PTS * (s + 1), lanes(f)]
            state_ref[PTS * c : PTS * (c + 1), lanes(f)] = 0.5 * (own_t + nbr_t) + 0.5 * (nbr_v - own_v)
    high, low = halves(state_ref[...])
    pick = one_hot(iota((FACES * E, faces_row.shape[1]), 0) == faces_row)
    return dot(high, pick) + dot(low, pick)


def column_of(row):
    count = row.shape[1]
    diagonal = iota((count, count), 0) == iota((count, count), 1)
    return jnp.sum(jnp.where(diagonal, row.astype(F32), 0.0), axis=1, keepdims=True)


def owner_masks(owner_row, gy_size):
    count = owner_row.shape[1]
    owner_col = column_of(owner_row)
    same = owner_col == owner_row.astype(F32)
    earlier = iota((count, count), 0) < iota((count, count), 1)
    rank = jnp.sum(jnp.where(same & earlier, 1.0, 0.0), axis=0, keepdims=True)
    named = iota((gy_size, count), 0) == owner_row
    return named, rank


def slot_values(params_ref, named, rank):
    out = []
    for c in range(3):
        both = []
        for r in range(2):
            col = params_ref[:, 3 * r + c : 3 * r + c + 1]
            both.append(jnp.sum(jnp.where(named, col, 0.0), axis=0, keepdims=True))
        out.append(jnp.where(rank > 0.5, both[1], both[0]))
    return out


def friction(state, slip, cohesion, flag):
    coeff = 0.6 - 0.3 * jnp.minimum(slip / 0.5, 1.0)
    normal, first, second = (state[PTS * c : PTS * (c + 1)] for c in range(3))
    strength = cohesion + coeff * jnp.maximum(-normal, 0.0)
    magnitude = jnp.sqrt(first * first + second * second)
    ratio = jnp.where(flag > 0.5, strength / jnp.maximum(magnitude, strength), 1.0)
    change = jnp.concatenate([first * (ratio - 1.0), second * (ratio - 1.0)], axis=0)
    slip_new = slip + jnp.sum(magnitude * (1.0 - ratio), axis=0, keepdims=True) / FACE_PTS
    return change, slip_new


def spread_change(change, faces_row):
    count = faces_row.shape[1]
    faces_col = column_of(faces_row)
    place = one_hot(iota((count, FACES * E), 1).astype(F32) == faces_col)
    high, low = halves(change)
    return dot(high, place) + dot(low, place)


def mix_faces(mats_ref, trace, start, flux_ref):
    def body(v, carry):
        cols = pl.ds(pl.multiple_of(v * E, E), E)
        for f in range(FACES):
            rows = slice(PTS * f, PTS * (f + 1))
            total = None if start is None else start[rows, cols]
            for w in range(VARS):
                term = mats_ref[v, w, f : f + 1, :] * trace(f, w)
                total = term if total is None else total + term
            flux_ref[rows, cols] = total
        return carry

    lax.fori_loop(0, VARS, body, 0)


def lift(lift_ref, flux_ref, out_ref):
    top = lift_ref[0][:, 0 : FACES * PTS]
    rest = lift_ref[1][:, 0 : FACES * PTS]
    for start in range(0, WIDE, 256):
        cols = slice(start, min(start + 256, WIDE))
        high, low = halves(flux_ref[:, cols])
        out_ref[:, cols] = dot(top, high) + (dot(top, low) + dot(rest, high))


def add_change(flux_ref, delta):
    for c, v in ((0, 3), (1, 5)):
        for f in range(FACES):
            rows = slice(PTS * f, PTS * (f + 1))
            flux_ref[rows, lanes(v)] = flux_ref[rows, lanes(v)] + delta[PTS * c : PTS * (c + 1), lanes(f)]


def plastic(read, mask_row, yield_row):
    q = [read(v) for v in range(6)]
    mean = (q[0] + q[1] + q[2]) / 3.0
    dev = [x - mean for x in q[0:3]]
    dev_sq = dev[0] * dev[0] + dev[1] * dev[1] + dev[2] * dev[2]
    shear_sq = q[3] * q[3] + q[4] * q[4] + q[5] * q[5]
    second = jnp.sum(dev_sq + 2.0 * shear_sq, axis=0, keepdims=True) / (2.0 * MODES)
    equiv = jnp.sqrt(second + 1e-06)
    factor = 1.0 - mask_row.astype(F32) * 0.5 * jnp.maximum(1.0 - yield_row / equiv, 0.0)
    return [mean + factor * x for x in dev] + [factor * x for x in q[3:6]]


def params_kernel(count, *refs):
    inputs, out_ref, passed = refs[0 : 3 + count], refs[3 + count], refs[4 + count : 4 + 2 * count]
    slots, sems = refs[4 + 2 * count : 7 + 2 * count], refs[7 + 2 * count :]
    copies = [pltpu.make_async_copy(*each) for each in zip(inputs, (*slots, *passed), sems)]
    for copy in copies:
        copy.start()
    for copy in copies[0:3]:
        copy.wait()
    slip_ref, cohesion_ref, flag_ref = slots
    gy_size = out_ref.shape[0]
    shape = (gy_size, slip_ref.shape[1])
    cols = []
    for r in range(2):
        mine = iota(shape, 1) == 2 * iota(shape, 0) + r
        for row in (slip_ref[...], cohesion_ref[...], flag_ref[...].astype(F32)):
            cols.append(jnp.sum(jnp.where(mine, row, 0.0), axis=1, keepdims=True))
    column = iota(out_ref.shape, 1)
    out = jnp.zeros(out_ref.shape, F32)
    for i, col in enumerate(cols):
        out = jnp.where(column == i, col, out)
    out_ref[...] = out
    for copy in copies[3:]:
        copy.wait()


def slip_kernel(in_ref, out_ref):
    shape = (in_ref.shape[0], out_ref.shape[1])
    out = jnp.zeros((1, shape[1]), F32)
    for r in range(2):
        mine = iota(shape, 1) == 2 * iota(shape, 0) + r
        out = out + jnp.sum(jnp.where(mine, in_ref[:, r : r + 1], 0.0), axis=0, keepdims=True)
    out_ref[...] = out


def first_kernel(
    stiff_ref, wave_ref, star_ref, proj_ref, send_ref,
    early_ref, late_ref, own_ref, high_ref, low_ref, m0, m1, m2, m3, ap_ref, at_ref,
    tall_a, tall_b, lhs_ref, square_ref, table_ref,
):
    ap_ref[...] = stack_stiffness(stiff_ref, lhs_ref)
    spread_faces(proj_ref, square_ref)
    at_ref[...] = widen(square_ref[0 : FACES * PTS])
    predict(wave_ref, star_ref, ap_ref[...], (tall_a, tall_b), early_ref, late_ref)
    make_traces(at_ref[...], early_ref, own_ref, table_ref, high_ref, low_ref)
    make_messages(send_ref, high_ref, low_ref, (m0, m1, m2, m3))


def volume_work(integral_ref, star_ref, left, vol_ref, tall_ref):
    product_of(left, lambda w: integral_ref[w], tall_ref)
    for pair in PAIRS:
        for v, total in zip(pair, star_mix(star_ref, tall_ref, pair)):
            vol_ref[v] = total


def near_work(own_mats_ref, own_ref, high_ref, low_ref, source_ref, flux_ref, near_ref):
    mix_faces(own_mats_ref, lambda f, w: own_ref[PTS * f : PTS * (f + 1), lanes(w)], None, flux_ref)
    for f in range(FACES):
        pick = one_hot(iota((FACES * E, E), 0) == source_ref[f : f + 1, :])
        near_ref[:, lanes(f)] = dot(high_ref[...], pick) + dot(low_ref[...], pick)


def near_first_kernel(
    integral_ref, star_ref, own_mats_ref, own_ref, high_ref, low_ref, source_ref, stiff_ref, lift_ref,
    vol_ref, flux_ref, near_ref, av_ref, al_ref,
    tall_ref, lhs_ref, square_ref,
):
    av_ref[...] = stack_stiffness_t(stiff_ref, lhs_ref, square_ref)
    spread_faces(lift_ref, square_ref)
    high, low = halves(jnp.transpose(square_ref[...])[0:MODES])
    al_ref[0] = high
    al_ref[1] = low
    volume_work(integral_ref, star_ref, av_ref[...], vol_ref, tall_ref)
    near_work(own_mats_ref, own_ref, high_ref, low_ref, source_ref, flux_ref, near_ref)


def middle_kernel(
    wave_hbm, late_ref, vol_ref, part_ref, near_ref, own_ref, m0, m1, m2, m3, nbr_mats_ref, source_ref,
    faces_ref, owner_ref, params_ref, star_ref, ap_ref, at_ref, al_ref, send_ref, cluster_ref, yield_ref, mask_ref,
    integral_ref, base_ref, own2_ref, high_ref, low_ref, n0, n1, n2, n3, par_ref,
    nbr_ref, state_ref, flux_ref, lifted_ref, mid_ref, tall_a, tall_b, table_ref, wave_ref, sem,
):
    copy = pltpu.make_async_copy(wave_hbm, wave_ref, sem)
    copy.start()
    finish_gather(source_ref, (m0, m1, m2, m3), near_ref, nbr_ref)
    faces_row = faces_ref[...]
    state = face_state(own_ref, nbr_ref, faces_row, state_ref)
    named, rank = owner_masks(owner_ref[...], params_ref.shape[0])
    slip, cohesion, flag = slot_values(params_ref, named, rank)
    change, slip_new = friction(state, slip, cohesion, flag)
    par_ref[0:1, :] = slip_new
    par_ref[1:2, :] = cohesion
    par_ref[2:3, :] = flag
    delta = spread_change(change, faces_row)
    mix_faces(
        nbr_mats_ref, lambda f, w: nbr_ref[PTS * w : PTS * (w + 1), lanes(f)], part_ref, flux_ref
    )
    add_change(flux_ref, delta)
    lift(al_ref, flux_ref, lifted_ref)
    copy.wait()
    coarse = cluster_ref[...] == 1
    for v in range(VARS):
        increment = vol_ref[v] - lifted_ref[:, lanes(v)]
        mid_ref[v] = wave_ref[v] + increment
        base_ref[v] = jnp.where(coarse, increment, 0.0)
    stressed = plastic(lambda v: mid_ref[v], mask_ref[...], yield_ref[...])
    for v in range(VARS):
        fine = stressed[v] if v < 6 else mid_ref[v]
        midway = jnp.where(coarse, wave_ref[v], fine)
        mid_ref[v] = midway
        base_ref[v] = midway + base_ref[v]
    predict(mid_ref, star_ref, ap_ref[...], (tall_a, tall_b), integral_ref, None)
    for v in range(VARS):
        integral_ref[v] = jnp.where(coarse, late_ref[v], integral_ref[v])
    make_traces(at_ref[...], integral_ref, own2_ref, table_ref, high_ref, low_ref)
    make_messages(send_ref, high_ref, low_ref, (n0, n1, n2, n3))


def fault_kernel(
    near_ref, own_ref, m0, m1, m2, m3, source_ref, faces_ref, owner_ref, params_ref, par_ref,
    nbr_ref, delta_ref, back_ref,
    state_ref,
):
    finish_gather(source_ref, (m0, m1, m2, m3), near_ref, nbr_ref)
    faces_row = faces_ref[...]
    state = face_state(own_ref, nbr_ref, faces_row, state_ref)
    change, slip_new = friction(state, par_ref[0:1, :], par_ref[1:2, :], par_ref[2:3, :])
    delta_ref[...] = spread_change(change, faces_row)
    named, rank = owner_masks(owner_ref[...], params_ref.shape[0])
    column = iota(back_ref.shape, 1)
    out = jnp.zeros(back_ref.shape, F32)
    for r in range(2):
        here = named & ((rank > 0.5) == (r == 1))
        total = jnp.sum(jnp.where(here, slip_new, 0.0), axis=1, keepdims=True)
        used = jnp.sum(jnp.where(here, 1.0, 0.0), axis=1, keepdims=True)
        value = jnp.where(used > 0.5, total, params_ref[:, 3 * r : 3 * r + 1])
        out = jnp.where(column == r, value, out)
    back_ref[...] = out


def last_kernel(
    star_hbm, base_ref, integral_ref, av_ref, part_ref, nbr_ref, delta_ref, nbr_mats_ref, al_ref, yield_ref, mask_ref,
    out_ref,
    vol_ref, tall_ref, flux_ref, lifted_ref, star_ref, sem,
):
    copy = pltpu.make_async_copy(star_hbm, star_ref, sem)
    copy.start()
    mix_faces(
        nbr_mats_ref, lambda f, w: nbr_ref[PTS * w : PTS * (w + 1), lanes(f)], part_ref, flux_ref
    )
    copy.wait()
    volume_work(integral_ref, star_ref, av_ref[...], vol_ref, tall_ref)
    add_change(flux_ref, delta_ref[...])
    lift(al_ref, flux_ref, lifted_ref)
    for v in range(VARS):
        out_ref[v] = base_ref[v] + (vol_ref[v] - lifted_ref[:, lanes(v)])
    stressed = plastic(lambda v: out_ref[v], mask_ref[...], yield_ref[...])
    for v in range(6):
        out_ref[v] = stressed[v]


def in_hbm(x):
    return pltpu.with_memory_space_constraint(x, pltpu.HBM)


def shape(dims, dtype=F32):
    return jax.ShapeDtypeStruct(dims, dtype)


def call(kernel, outs, scratch=(), hbm=0):
    in_vmem = pl.BlockSpec(memory_space=pltpu.VMEM)
    from_hbm = pl.BlockSpec(memory_space=pltpu.HBM)
    many = isinstance(outs, list)

    def run(*args):
        return pl.pallas_call(
            kernel,
            out_shape=outs,
            in_specs=[from_hbm] * hbm + [in_vmem] * (len(args) - hbm),
            out_specs=[in_vmem] * len(outs) if many else in_vmem,
            scratch_shapes=[pltpu.VMEM(dims, dtype) for dims, dtype in scratch] + [pltpu.SemaphoreType.DMA] * hbm,
            compiler_params=pltpu.CompilerParams(vmem_limit_bytes=LIMIT),
        )(*args)

    return run


FIELD = (VARS, MODES, E)
TRACE = (FACES * PTS, WIDE)
TABLE = (ROWS, FACES * E)
LEFT = (3 * MODES, 256)
TALL = (3 * MODES, WIDE)


def pair_up(x, axis, odd):
    count = lax.axis_size(axis)
    if odd:
        pairs = [(i, (i + 1) % count if i % 2 else (i - 1) % count) for i in range(count)]
    else:
        pairs = [(i, i ^ 1) for i in range(count)]
    return lax.ppermute(x, axis, pairs)


EDGES = (("gx", 0), ("gx", 1), ("gy", 0), ("gy", 1))


def exchange(messages):
    received = []
    for x, (axis, odd) in zip(messages, EDGES):
        received.append(pair_up(x, axis, odd))
    return received


def local(
    wavefield,
    star_mats,
    flux_own,
    flux_nbr,
    stiffness,
    face_proj,
    lift_mats,
    cluster,
    yield_stress,
    plastic_mask,
    face_source,
    send_faces,
    fault_faces,
    fault_owner,
    fault_slip,
    cohesion,
    slip_flag,
):
    gy_size = lax.axis_size("gy")
    faults = fault_faces.shape[1]
    slot_count = fault_slip.shape[0]
    star = jnp.transpose(star_mats, (1, 2, 0, 3))
    own_mats = jnp.transpose(flux_own, (1, 2, 0, 3))
    nbr_mats = jnp.transpose(flux_nbr, (1, 2, 0, 3))
    proj = jnp.transpose(face_proj, (1, 0, 2))
    lifts = jnp.transpose(lift_mats, (2, 0, 1))
    owner = jnp.transpose(fault_owner)
    cluster, yield_stress, plastic_mask = (x.reshape(1, E) for x in (cluster, yield_stress, plastic_mask))
    slots = [x.reshape(1, slot_count) for x in (fault_slip, cohesion, slip_flag)]

    small = (send_faces, face_source, fault_faces, owner, cluster, yield_stress, plastic_mask)
    firsts = (stiffness, wavefield, star, proj, *small)
    params, *brought = call(
        lambda *refs: params_kernel(len(firsts), *refs),
        [shape((gy_size, 8)), *(shape(x.shape, x.dtype) for x in firsts)],
        [(x.shape, x.dtype) for x in slots],
        hbm=3 + len(firsts),
    )(*(in_hbm(x) for x in (*slots, *firsts)))
    stiffness, wave_first, star_first, proj = brought[0:4]
    send_faces, face_source, fault_faces, owner, cluster, yield_stress, plastic_mask = brought[4:]
    params = lax.all_to_all(params, "gy", 0, 0, tiled=True)

    messages = [shape((MSG, E))] * 4
    work = [(TALL, F32), (TALL, F32)]
    early, late, own, high, low, m0, m1, m2, m3, ap, at = call(
        first_kernel,
        [shape(FIELD), shape(FIELD), shape(TRACE), shape(TABLE, BF16), shape(TABLE, BF16), *messages,
         shape(LEFT, BF16), shape((FACES * PTS, 256), BF16)],
        work + [((3 * MODES, E), F32), ((E, E), F32), (TABLE, F32)],
    )(stiffness, wave_first, star_first, proj, send_faces)
    got = exchange((m0, m1, m2, m3))
    vol, part, near, av, al = call(
        near_first_kernel,
        [shape(FIELD), shape(TRACE), shape(TABLE), shape(LEFT, BF16), shape((2, MODES, E), BF16)],
        work[1:] + [((3 * MODES, E), F32), ((E, E), F32)],
    )(early, star, own_mats, own, high, low, face_source, stiffness, lifts)
    integral, base, own, high, low, m0, m1, m2, m3, par = call(
        middle_kernel,
        [shape(FIELD), shape(FIELD), shape(TRACE), shape(TABLE, BF16), shape(TABLE, BF16), *messages,
         shape((8, faults))],
        [(TABLE, F32), ((3 * PTS + 8, FACES * E), F32), (TRACE, F32), ((MODES, WIDE), F32), (FIELD, F32)]
        + work + [(TABLE, F32), (FIELD, F32)],
        hbm=1,
    )(in_hbm(wavefield), late, vol, part, near, own, *got, nbr_mats, face_source, fault_faces, owner, params, star,
      ap, at, al, send_faces, cluster, yield_stress, plastic_mask)
    got = exchange((m0, m1, m2, m3))
    part, near = call(near_work, [shape(TRACE), shape(TABLE)])(own_mats, own, high, low, face_source)
    nbr, delta, back = call(
        fault_kernel,
        [shape(TABLE), shape((2 * PTS, FACES * E)), shape((gy_size, 8))],
        [((3 * PTS + 8, FACES * E), F32)],
    )(near, own, *got, face_source, fault_faces, owner, params, par)
    back = lax.all_to_all(back, "gy", 0, 0, tiled=True)
    out = call(
        last_kernel,
        shape(FIELD),
        [(FIELD, F32), (TALL, F32), (TRACE, F32), ((MODES, WIDE), F32), (star.shape, F32)],
        hbm=1,
    )(in_hbm(star), base, integral, av, part, nbr, delta, nbr_mats, al, yield_stress, plastic_mask)
    slip_out = call(slip_kernel, shape((1, slot_count)))(back)
    return (out, slip_out.reshape(slot_count))


def solution(mesh):
    flat = ("gx", "gy")
    last2, last3, last1 = P(None, None, flat), P(None, None, None, flat), P(flat)

    return jax.shard_map(
        local,
        mesh=mesh,
        in_specs=(
            last2, last3, last3, last3, P(), P(), P(), last1, last1, last1,
            P(None, flat), P(flat, None), P(flat, None), P(flat, None), last1, last1, last1,
        ),
        out_specs=(last2, last1),
        check_vma=False,
    )
```
